32 devices in a mesh: gx: 8 (over y, x, core), gy: 4 (over z).
Axes of the slice: x: 2, y: 2, z: 4, core: 2. Of those that a mesh axis runs over, the one named last changes fastest.
Arguments:
- initial: float32 [3, 48, 64, 1024], P(None, None, 'gy', 'gx'), may hold values from -6 to 6
- sectioned: float32 [3, 48, 64, 1024], P(None, None, 'gy', 'gx'), may hold values from -6 to 6
- rotor_faces: int32 [4, 256], P('gy', 'gx'), may hold values from 0 to 191, as said below
- intersections: int32 [4, 1024, 3], P('gy', 'gx'), may hold values from 0 to 255, as said below
- live_counts: int32 [4, 8], P('gy', 'gx'), may hold values from 2 to 128, as said below
- mortar_blocks: float32 [16, 64, 64], replicated, may hold values from -0.5 to 0.5
Outputs:
- advanced: float32 [3, 48, 64, 1024], P(None, None, 'gy', 'gx')
The draws below stay inside these ranges and needn't reach their ends.
Inputs may be any that keep to these rules, and one draw needn't show every extreme that they name: `rotor_faces`: 32 distinct local face ids on each device, below 192. `intersections`: on each device, entries 2j and 2j + 1 name the same stator face, and the 64 stator faces of a device are distinct; the rotor index is a row of the device row's table (below 256); the block is below 16. `live_counts`: Even; the first live_count entries of a device's list are live, the rest are ignored.
All inputs are finite; a program needn't handle non-finite values.
Results may differ from the reference program's by a relative error of at most 0.0003.
Values sent between devices are 32-bit elements; how exact they have to be, the bound alone decides.
A program may use at most 128 MiB of HBM per device.

```python
import jax
import jax.numpy as jnp
import numpy as np
from jax import lax

EX = 16
EY = 2
EZ = 6
R = 32
S = 64
NB = 16
DEV_X = 8
DEV_Y = 4
CYCLE = 256
N_GX = 8
N_GY = 4


def first_faces(base_key, wanted):
    key_list = jax.random.split(base_key, DEV_Y * DEV_X)
    return jax.vmap(lambda single: jax.random.permutation(single, EZ * EY * EX)[:wanted])(key_list)


def draw_rotor_faces(key, part):
    picked = first_faces(jax.random.fold_in(key, 11), R)
    return picked.reshape(DEV_Y, DEV_X * R).astype(jnp.int32)


def draw_intersections(key, part):
    key_list = jax.random.split(jax.random.fold_in(key, 23), 3)
    stators = first_faces(key_list[0], S)
    sources = jax.random.randint(key_list[1], (DEV_Y * DEV_X, S), 0, CYCLE)
    chosen = jax.random.randint(key_list[2], (DEV_Y * DEV_X, S, 2), 0, NB)
    first_entry = jnp.stack((stators, sources, chosen[..., 0]), -1)
    second_entry = jnp.stack((stators, (sources + 1) % CYCLE, chosen[..., 1]), -1)
    paired = jnp.stack((first_entry, second_entry), 2)
    return paired.reshape(DEV_Y, DEV_X * 2 * S, 3).astype(jnp.int32)


def draw_live_counts(key, part):
    row_ids = jnp.arange(DEV_Y, dtype=jnp.int32)[:, None]
    busy_rows = (row_ids >= DEV_Y * 3 // 8) & (row_ids < DEV_Y * 5 // 8)
    light_load = jax.random.randint(jax.random.fold_in(key, 37), (DEV_Y, DEV_X), 1, S + 1)
    return (2 * jnp.where(busy_rows, S, light_load)).astype(jnp.int32)


def block_levels(own_key, extent, shards, least, high):
    def one(axis_at, parts):
        heights = jax.random.uniform(jax.random.fold_in(jax.random.fold_in(own_key, 6), axis_at), (parts,), jnp.float32, least / len(shards), high / len(shards))
        return jnp.repeat(jnp.exp(heights), extent[axis_at] // parts).reshape((-1,) + (1,) * (len(extent) - axis_at - 1))

    level = one(*shards[0])
    for cut in shards[1:]:
        level = level * one(*cut)
    return level


def noise(rng, dims, scale, bound, shards=(), kind=jnp.bfloat16):
    values = scale * jax.random.normal(rng, dims, jnp.float32)
    if shards:
        values = values * block_levels(rng, dims, shards, -0.22, 0.18)
    return jnp.clip(values, -bound, bound).astype(kind)


def setup_inputs(seed: int = 0) -> dict:
    splits = jax.random.split(jax.random.key(seed), 7)
    initial = noise(splits[0], (3, 8 * EZ, 8 * EY * N_GY, 8 * EX * N_GX), 1.0, 6.0, ((2, 4), (3, 8)), jnp.float32)
    sectioned = noise(splits[1], (3, 8 * EZ, 8 * EY * N_GY, 8 * EX * N_GX), 1.0, 6.0, ((2, 4), (3, 8)), jnp.float32)
    rotor_faces = draw_rotor_faces(jax.random.fold_in(splits[6], 71), 0)
    intersections = draw_intersections(jax.random.fold_in(splits[6], 71), 0)
    live_counts = draw_live_counts(jax.random.fold_in(splits[6], 71), 0)
    mortar_blocks = noise(splits[5], (NB, 64, 64), 128 ** -0.5, 0.5, (), jnp.float32)
    return dict(initial=initial, sectioned=sectioned, rotor_faces=rotor_faces, intersections=intersections, live_counts=live_counts, mortar_blocks=mortar_blocks)


time_step = 0.02
viscosity = 0.005
smagorinsky = 0.002
gll_interior = [-0.8717401485096066, -0.5917001814331423, -0.2092992179024789, 0.2092992179024789, 0.5917001814331423, 0.8717401485096066]

def legendre_seven(points):
    lower_poly = points * 0.0 + 1.0
    current = points * 1.0
    for order_at in range(1, 7):
        following = ((2 * order_at + 1) * points * current - order_at * lower_poly) / (order_at + 1)
        lower_poly = current
        current = following
    return current

def gll_tables():
    degree = 7
    points = np.array([-1.0] + gll_interior + [1.0])
    values = legendre_seven(points)
    slope_table = np.zeros((degree + 1, degree + 1))
    for row_at in range(degree + 1):
        for col_at in range(degree + 1):
            if row_at != col_at:
                slope_table[row_at, col_at] = values[row_at] / (values[col_at] * (points[row_at] - points[col_at]))
    slope_table[0, 0] = -degree * (degree + 1) / 4.0
    slope_table[degree, degree] = degree * (degree + 1) / 4.0
    return (slope_table, slope_table @ slope_table)

def derive(grid_field, direction, table):
    moved = jnp.moveaxis(grid_field, direction, -1)
    shaped = moved.reshape(moved.shape[:-1] + (moved.shape[-1] // 8, 8))
    result = jnp.einsum('...k,jk->...j', shaped, table, precision=lax.Precision.HIGHEST)
    return jnp.moveaxis(result.reshape(moved.shape), -1, direction)

def tendency(velocity, slope_table, curve_table):
    slope_matrix = jnp.asarray(slope_table, jnp.float32)
    curve_matrix = jnp.asarray(curve_table, jnp.float32)
    gradient = [derive(velocity, direction, slope_matrix) for direction in (3, 2, 1)]
    advection = velocity[0:1] * gradient[0] + velocity[1:2] * gradient[1] + velocity[2:3] * gradient[2]
    strain_sq = jnp.zeros(velocity.shape[1:], jnp.float32)
    for comp_one in range(3):
        for comp_two in range(3):
            strain_part = 0.5 * (gradient[comp_two][comp_one] + gradient[comp_one][comp_two])
            strain_sq = strain_sq + strain_part * strain_part
    eddy_rate = viscosity + smagorinsky * jnp.sqrt(2.0 * strain_sq + 1e-06)
    laplace = derive(velocity, 3, curve_matrix) + derive(velocity, 2, curve_matrix) + derive(velocity, 1, curve_matrix)
    return eddy_rate * laplace - advection

def pad_one(grid_field, direction):
    widths = [(0, 0)] * grid_field.ndim
    widths[direction] = (1, 1)
    return jnp.pad(grid_field, widths)

def pair_average(padded, direction, start, total):
    length = padded.shape[direction] - 2
    center = lax.slice_in_dim(padded, 1, length + 1, axis=direction)
    lower = lax.slice_in_dim(padded, 0, length, axis=direction)
    upper = lax.slice_in_dim(padded, 2, length + 2, axis=direction)
    position = start + jnp.arange(length, dtype=jnp.int32)
    shape_one = [1] * padded.ndim
    shape_one[direction] = length
    take_lower = ((position % 8 == 0) & (position > 0)).reshape(shape_one)
    take_upper = ((position % 8 == 7) & (position < total - 1)).reshape(shape_one)
    return jnp.where(take_lower, 0.5 * (center + lower), jnp.where(take_upper, 0.5 * (center + upper), center))

def global_faces(grid_field):
    picked = grid_field.reshape(3, EZ, 8, DEV_Y, EY, 8, DEV_X, EX, 8)[..., 0]
    return picked.transpose(3, 6, 1, 4, 7, 0, 2, 5).reshape(DEV_Y, DEV_X, EZ * EY * EX, 192)

def put_faces(grid_field, face_rows):
    blocks = face_rows.reshape(DEV_Y, DEV_X, EZ, EY, EX, 3, 8, 8).transpose(5, 2, 6, 0, 3, 7, 1, 4)
    spread = grid_field.reshape(3, EZ, 8, DEV_Y, EY, 8, DEV_X, EX, 8).at[..., 0].set(blocks)
    return spread.reshape(grid_field.shape)

def mortar_faces(face_rows, table_rows, entries, count, blocks):
    stator = entries[:, 0]
    source = entries[:, 1]
    chosen = entries[:, 2]
    live_mask = jnp.arange(entries.shape[0], dtype=jnp.int32) < count
    incoming = table_rows[source].reshape(entries.shape[0], 3, 64)

    def apply_block(carried, block_id):
        product = jnp.einsum('eci,ji->ecj', incoming, blocks[block_id], precision=lax.Precision.HIGHEST)
        return (jnp.where((chosen == block_id)[:, None, None], product, carried), None)
    projected, unused = lax.scan(apply_block, jnp.zeros(incoming.shape, jnp.float32), jnp.arange(blocks.shape[0], dtype=jnp.int32))
    projected = jnp.where(live_mask[:, None, None], projected, 0.0).reshape(entries.shape[0], 192)
    summed = jax.ops.segment_sum(projected, stator, num_segments=face_rows.shape[0])
    touched = jax.ops.segment_sum(live_mask.astype(jnp.int32), stator, num_segments=face_rows.shape[0]) > 0
    return jnp.where(touched[:, None], 0.5 * (face_rows + summed), face_rows)

def reference(initial, sectioned, rotor_faces, intersections, live_counts, mortar_blocks):
    slope_table, curve_table = gll_tables()
    depth, height, width = (sectioned.shape[1], sectioned.shape[2], sectioned.shape[3])
    row_height = height // DEV_Y
    stacked = sectioned.reshape(3, depth, DEV_Y, row_height, width).transpose(2, 0, 1, 3, 4)
    rates = lax.map(lambda block_rows: tendency(block_rows, slope_table, curve_table), stacked)
    rates = rates.transpose(1, 2, 0, 3, 4).reshape(sectioned.shape)
    merged = pair_average(pad_one(rates, 3), 3, 0, width)
    merged = pair_average(pad_one(merged, 2), 2, 0, height)
    merged = pair_average(pad_one(merged, 1), 1, 0, depth)
    rate_rows = global_faces(rates)
    merged_rows = global_faces(merged)
    face_ids = rotor_faces.reshape(DEV_Y, DEV_X, R)
    panels = jax.vmap(jax.vmap(lambda face_table, picks: face_table[picks]))(rate_rows, face_ids)
    row_tables = panels.reshape(DEV_Y, CYCLE, 192)
    device_tables = jnp.broadcast_to(row_tables[:, None], (DEV_Y, DEV_X, CYCLE, 192))
    entries = intersections.reshape(DEV_Y, DEV_X, 2 * S, 3)
    inner = jax.vmap(mortar_faces, in_axes=(0, 0, 0, 0, None))
    updated = jax.vmap(inner, in_axes=(0, 0, 0, 0, None))(merged_rows, device_tables, entries, live_counts, mortar_blocks)
    final = put_faces(merged, updated)
    return initial * (1.0 / 3.0) + 2.0 / 3.0 * (sectioned + time_step * final)
```

```python
import functools

import jax
import jax.numpy as jnp
import numpy as np
from jax import lax
from jax.experimental import pallas as pl
from jax.experimental.pallas import tpu as pltpu
from jax.sharding import PartitionSpec as P

time_step = 0.02
viscosity = 0.005
smagorinsky = 0.002
gll_interior = [
    -0.8717401485096066,
    -0.5917001814331423,
    -0.2092992179024789,
    0.2092992179024789,
    0.5917001814331423,
    0.8717401485096066,
]


def legendre_seven(points):
    lower_poly = points * 0.0 + 1.0
    current = points * 1.0
    for order_at in range(1, 7):
        following = ((2 * order_at + 1) * points * current - order_at * lower_poly) / (order_at + 1)
        lower_poly = current
        current = following
    return current


def gll_tables():
    degree = 7
    points = np.array([-1.0] + gll_interior + [1.0])
    values = legendre_seven(points)
    slope_table = np.zeros((degree + 1, degree + 1))
    for row_at in range(degree + 1):
        for col_at in range(degree + 1):
            if row_at != col_at:
                slope_table[row_at, col_at] = values[row_at] / (
                    values[col_at] * (points[row_at] - points[col_at])
                )
    slope_table[0, 0] = -degree * (degree + 1) / 4.0
    slope_table[degree, degree] = degree * (degree + 1) / 4.0
    return (slope_table, slope_table @ slope_table)


F32 = jnp.float32
BF16 = jnp.bfloat16
MESH = pl.DeviceIdType.MESH
NT = (((1,), (1,)), ((), ()))
NN = (((1,), (0,)), ((), ()))


def split_table(table):
    table = np.asarray(table, np.float32)
    high = table.astype(BF16)
    return high, (table - high.astype(np.float32)).astype(BF16)


def operators(height, width):
    slope, curve = gll_tables()
    rows = np.eye(height // 8)
    left = np.concatenate(
        [
            np.kron(np.eye(8), np.kron(rows, slope)),
            np.kron(slope, np.eye(height)),
            np.kron(np.eye(8), np.kron(rows, curve)) + np.kron(curve, np.eye(height)),
        ]
    )
    high, low = split_table(left)
    left = np.concatenate([high, high, low], 1)
    cols = np.eye(width // 8)
    right = np.concatenate([np.kron(cols, slope).T, np.kron(cols, curve).T], 1)
    high, low = split_table(right)
    right = np.concatenate([high, high, low], 0)
    return left, right


def halves(value):
    high = value.astype(BF16)
    return high, (value - high.astype(F32)).astype(BF16)


def dot(left, right, dims=NN):
    return lax.dot_general(left, right, dims, preferred_element_type=F32)


def iota(shape, dim):
    return lax.broadcasted_iota(jnp.int32, shape, dim)


def step_kernel(
    across,
    along,
    sec_hbm,
    rotor_hbm,
    entry_hbm,
    count_hbm,
    mortar_hbm,
    left_hbm,
    right_hbm,
    start_hbm,
    out_ref,
    start_ref,
    sec_ref,
    rotor_ref,
    entry_ref,
    count_ref,
    mortar_ref,
    left_ref,
    right_ref,
    load_sem,
    sec_sem,
    yz_ref,
    x_ref,
    rate_ref,
    merged_ref,
    table_ref,
    edge_ref,
    edge_in_ref,
    row_ref,
    row_in_ref,
    weight_ref,
    spread_ref,
    panel_send,
    panel_recv,
    edge_send,
    edge_recv,
    row_send,
    row_recv,
):
    _, depth, height, width = sec_ref.shape
    layers, tall = depth // 8, height // 8
    plane = 8 * height
    columns = layers * tall * width
    slots = rotor_ref.shape[1]
    packed = slots // 2
    shift = packed.bit_length() - 1
    entries = entry_ref.shape[2]
    pairs = entries // 2
    blocks = mortar_ref.shape[0]
    gx = lax.axis_index("gx")
    gy = lax.axis_index("gy")
    has_x = (gx > 0, gx < across - 1)
    has_y = (gy > 0, gy < along - 1)

    def number(flag):
        return jnp.where(flag, 1, 0)

    group = 2 if layers % 2 == 0 else 1

    def sec_load(at):
        span = pl.ds(pl.multiple_of(at * group * 8, 8), group * 8)
        return pltpu.make_async_copy(sec_hbm.at[:, span], sec_ref.at[:, span], sec_sem.at[at])

    loads = [
        pltpu.make_async_copy(source, target, load_sem.at[i])
        for i, (source, target) in enumerate(
            [
                (left_hbm, left_ref),
                (right_hbm, right_ref),
                (rotor_hbm, rotor_ref),
                (entry_hbm, entry_ref),
                (count_hbm, count_ref),
                (mortar_hbm, mortar_ref),
                (start_hbm, start_ref),
            ]
        )
    ]
    sec_load(0).start()
    loads[0].start()
    loads[1].start()
    for at in range(1, layers // group):
        sec_load(at).start()
    for load in loads[2:]:
        load.start()

    barrier = pltpu.get_barrier_semaphore()
    for d in range(1, across):
        pl.semaphore_signal(
            barrier, inc=1, device_id={"gx": lax.rem(gx + d, across)}, device_id_type=MESH
        )
    for b in range(2):
        for dx in (-1, 0, 1):
            there = has_y[b] if dx == 0 else has_y[b] & has_x[(dx + 1) // 2]

            @pl.when(there)
            def _(b=b, dx=dx):
                pl.semaphore_signal(
                    barrier,
                    inc=1,
                    device_id={"gx": gx + dx, "gy": gy + 2 * b - 1},
                    device_id_type=MESH,
                )

    lane = iota((height, width), 1)
    y8 = lane & 7
    own = jnp.where((y8 == 0) | (y8 == 7), 0.5, 1.0)
    own = jnp.where((lane == 0) & jnp.logical_not(has_x[0]), 1.0, own)
    own = jnp.where((lane == width - 1) & jnp.logical_not(has_x[1]), 1.0, own)
    other = jnp.where(((y8 == 0) & (lane > 0)) | ((y8 == 7) & (lane < width - 1)), 0.5, 0.0)
    loads[0].wait()
    loads[1].wait()

    def layer_group(at, carry):
        sec_load(at).wait()
        for c in range(3):
            parts = [
                sec_ref[c, pl.ds((at * group + q) * 8, 8)].reshape(plane, width)
                for q in range(group)
            ]
            high, low = halves(jnp.concatenate(parts, 1))
            yz_ref[c] = dot(left_ref[...], jnp.concatenate([high, low, high], 0))
            high, low = halves(jnp.concatenate(parts, 0))
            x_ref[c] = dot(jnp.concatenate([high, low, high], 1), right_ref[...])
        for q in range(group):

            def level(z, carry2):
                rows = pl.multiple_of(z * height, height)
                z_at = (at * group + q) * 8 + z
                vel = [sec_ref[c, z_at] for c in range(3)]
                grad = [[], [], []]
                lap = []
                for c in range(3):
                    x_rows = pl.ds(q * plane + rows, height)
                    lanes = pl.ds(q * width, width)
                    grad[0].append(x_ref[c, x_rows, pl.ds(0, width)])
                    grad[1].append(yz_ref[c, pl.ds(rows, height), lanes])
                    grad[2].append(yz_ref[c, pl.ds(plane + rows, height), lanes])
                    lap.append(
                        x_ref[c, x_rows, pl.ds(width, width)]
                        + yz_ref[c, pl.ds(2 * plane + rows, height), lanes]
                    )
                strain = grad[0][0] * grad[0][0] + grad[1][1] * grad[1][1] + grad[2][2] * grad[2][2]
                for one, two in ((0, 1), (0, 2), (1, 2)):
                    both = grad[one][two] + grad[two][one]
                    strain = strain + 0.5 * (both * both)
                eddy = viscosity + smagorinsky * jnp.sqrt(2.0 * strain + 1e-06)
                for c in range(3):
                    rate = eddy * lap[c] - (
                        vel[0] * grad[0][c] + vel[1] * grad[1][c] + vel[2] * grad[2][c]
                    )
                    partner = jnp.where(
                        y8 == 0, pltpu.roll(rate, 1, 1), pltpu.roll(rate, width - 1, 1)
                    )
                    at_rows = pl.ds(pl.multiple_of((c * depth + z_at) * height, height), height)
                    rate_ref[at_rows, :] = rate
                    merged_ref[at_rows, :] = own * rate + other * partner
                return carry2

            lax.fori_loop(0, 8, level, 0, unroll=True)
        return carry

    lax.fori_loop(0, layers // group, layer_group, 0)

    for load in loads[2:6]:
        load.wait()

    line = 2 * packed + 32
    half_rows = packed + 16
    row_at = iota((line, slots), 0)
    place = row_at & (half_rows - 1) if half_rows & (half_rows - 1) == 0 else row_at % half_rows
    half_at = jnp.where(row_at >= half_rows, 1, 0)
    wanted = (place < packed) & (iota((line, slots), 1) == half_at * packed + place)
    faces = jnp.broadcast_to(rotor_ref[...].astype(F32), (line, slots))
    face = jnp.sum(jnp.where(wanted, faces, 0.0), axis=1, keepdims=True)
    row_one = iota((line, 1), 0)
    half_one = jnp.where(row_one >= half_rows, 1, 0)
    place_one = row_one - half_one * half_rows - packed
    layer_one = place_one & 7
    side_one = jnp.where(place_one >= 8, 1, 0)
    edge_to = (layer_one * tall + half_one) * width + side_one * (width - 1)
    edge_to = jnp.where(layer_one < layers, edge_to, -1)
    target = jnp.where(place_one < 0, 8.0 * face, edge_to.astype(F32))
    column = iota((line, columns), 1).astype(F32)
    pick = jnp.where(column == target, 1.0, 0.0).astype(BF16)
    low_lane = iota((half_rows, 128), 1) < 64
    for c in range(3):
        parts = []
        for k in range(layers):
            stack = rate_ref[pl.ds((c * depth + 8 * k) * height, plane), :].reshape(8, height, width)
            for j in range(tall):
                parts.append(stack[:, 8 * j : 8 * j + 8].reshape(64, width))
        value = jnp.concatenate(parts, 1)
        high, low = halves(jnp.concatenate([value, value], 0))
        found = dot(pick, high, NT) + dot(pick, low, NT)
        found = jnp.where(low_lane, found[:half_rows], found[half_rows:])
        table_ref[gx, c] = found[:packed]
        edge_ref[0, c] = found[packed : packed + 8]
        edge_ref[1, c] = found[packed + 8 :]

    for c in range(3):
        for k in range(1, layers):
            top = pl.ds((c * depth + 8 * k - 1) * height, height)
            bottom = pl.ds((c * depth + 8 * k) * height, height)
            mean = 0.5 * (merged_ref[top, :] + merged_ref[bottom, :])
            merged_ref[top, :] = mean
            merged_ref[bottom, :] = mean
    lines = 3 * depth

    def y_rows(y):
        return (pl.ds(y, lines, stride=height), slice(None))

    row_ref[0] = merged_ref[y_rows(0)]
    row_ref[1] = merged_ref[y_rows(height - 1)]

    expected = across - 1
    for b in range(2):
        expected = expected + number(has_y[b]) * (1 + number(has_x[0]) + number(has_x[1]))
    pl.semaphore_wait(barrier, expected)

    panel_copies = []
    for d in range(1, across):
        panel_copies.append(
            pltpu.make_async_remote_copy(
                src_ref=table_ref.at[gx],
                dst_ref=table_ref.at[gx],
                send_sem=panel_send.at[d - 1],
                recv_sem=panel_recv.at[d - 1],
                device_id={"gx": lax.rem(gx + d, across)},
                device_id_type=MESH,
            )
        )
        panel_copies[-1].start()

    def row_copy(b):
        return pltpu.make_async_remote_copy(
            src_ref=row_ref.at[b],
            dst_ref=row_in_ref.at[1 - b],
            send_sem=row_send.at[b],
            recv_sem=row_recv.at[1 - b],
            device_id={"gy": gy + 2 * b - 1},
            device_id_type=MESH,
        )

    def edge_copy(a, dy):
        return pltpu.make_async_remote_copy(
            src_ref=edge_ref.at[a],
            dst_ref=edge_in_ref.at[1 - a, 1 - dy],
            send_sem=edge_send.at[a, dy + 1],
            recv_sem=edge_recv.at[1 - a, 1 - dy],
            device_id={"gx": gx + 2 * a - 1, "gy": gy + dy},
            device_id_type=MESH,
        )

    def edge_there(a, dy):
        return has_x[a] if dy == 0 else has_x[a] & has_y[(dy + 1) // 2]

    edge_list = [(a, dy) for a in range(2) for dy in (-1, 0, 1)]
    for b in range(2):

        @pl.when(has_y[b])
        def _(b=b):
            row_copy(b).start()

    for a, dy in edge_list:

        @pl.when(edge_there(a, dy))
        def _(a=a, dy=dy):
            edge_copy(a, dy).start()

        @pl.when(jnp.logical_not(edge_there(a, dy)))
        def _(a=a, dy=dy):
            edge_in_ref[a, dy + 1] = jnp.zeros(edge_in_ref.shape[2:], F32)

    mean = 0.5 * (merged_ref[y_rows(7)] + merged_ref[y_rows(8)])
    merged_ref[y_rows(7)] = mean
    merged_ref[y_rows(8)] = mean

    depth_k = blocks * 64
    for p in range(blocks // 2):
        high, low = halves(jnp.concatenate([mortar_ref[2 * p], mortar_ref[2 * p + 1]], 1))
        weight_ref[:, pl.ds(p * 128, 128)] = high
        weight_ref[:, pl.ds(depth_k + p * 128, 128)] = high
        weight_ref[:, pl.ds(2 * depth_k + p * 128, 128)] = low

    entry_lane = iota((pairs, entries), 1)
    entry_row = 2 * iota((pairs, entries), 0)

    def upright(kind, odd_one):
        values = jnp.broadcast_to(entry_ref[kind].astype(F32), (pairs, entries))
        values = jnp.where(entry_lane == entry_row + odd_one, values, 0.0)
        return jnp.sum(values, axis=1, keepdims=True).astype(jnp.int32)

    live = 2 * iota((pairs, 1), 0) < count_ref[...]
    stator = jnp.where(live, 8 * upright(0, 0), -1)
    spread = jnp.where(iota((pairs, columns), 1) == stator, 0.5, 0.0)
    factor = 1.0 - jnp.max(spread, axis=0, keepdims=True)
    spread_ref[pl.ds(0, pairs), :] = spread.astype(BF16)
    spread_ref[pl.ds(pairs, pairs), :] = spread.astype(BF16)
    row_e = iota((128, 1), 0)
    layer_e = row_e & 7
    side_e = (row_e >> 4) & 1
    tall_e = row_e >> 5
    kept = (tall_e < tall) & (layer_e < layers)
    kept = kept & (jnp.where(side_e == 0, number(has_x[0]), number(has_x[1])) > 0)
    to_e = jnp.where(kept, (layer_e * tall + tall_e) * width + side_e * (width - 1), -1)
    spread_ref[pl.ds(2 * pairs, 128), :] = jnp.where(
        iota((128, columns), 1) == to_e, 0.5 * factor, 0.0
    ).astype(BF16)

    lane_half = iota((pairs, 128), 1) >> 6
    chosen = [jnp.where(live, upright(2, odd_one), -1) for odd_one in (0, 1)]
    source = jnp.concatenate([upright(1, 0), upright(1, 1)], 0)
    spots = across * packed
    table_row = iota((2 * pairs, spots), 1)
    first_id = table_row + ((table_row >> shift) << shift)
    gather = jnp.where((source == first_id) | (source == first_id + packed), 1.0, 0.0).astype(BF16)
    source_half = (source >> shift) & 1
    take = jnp.where((iota((64, 128), 1) & 63) == iota((64, 128), 0), 1.0, 0.0).astype(BF16)

    e_lane = iota((8, 128), 1)
    e_row = iota((8, 128), 0)
    e_y = e_lane & 7
    e_z = (e_lane >> 3) & 7
    e_low = e_lane < 64
    for a, dy in edge_list:

        @pl.when(edge_there(a, dy))
        def _(a=a, dy=dy):
            pltpu.make_async_remote_copy(
                src_ref=edge_ref.at[a],
                dst_ref=edge_in_ref.at[a, dy + 1],
                send_sem=edge_send.at[a, dy + 1],
                recv_sem=edge_recv.at[a, dy + 1],
                device_id={"gx": gx + 2 * a - 1, "gy": gy + dy},
                device_id_type=MESH,
            ).wait()

    y_move = ((e_y == 0) & (jnp.logical_not(e_low) | has_y[0])) | (
        (e_y == 7) & (e_low | has_y[1])
    )
    z_move = ((e_z == 0) & (e_row > 0)) | ((e_z == 7) & (e_row < layers - 1))
    spans = []
    for c in range(3):
        stack = []
        for a in range(2):
            mid = edge_in_ref[a, 1, c]
            near = jnp.where(
                e_y == 0,
                jnp.where(e_low, pltpu.roll(edge_in_ref[a, 0, c], 57, 1), pltpu.roll(mid, 57, 1)),
                jnp.where(e_low, pltpu.roll(mid, 71, 1), pltpu.roll(edge_in_ref[a, 2, c], 71, 1)),
            )
            mid = jnp.where(y_move, 0.5 * (mid + near), mid)
            near = jnp.where(
                e_z == 0,
                pltpu.roll(pltpu.roll(mid, 72, 1), 1, 0),
                pltpu.roll(pltpu.roll(mid, 56, 1), 7, 0),
            )
            mid = jnp.where(z_move, 0.5 * (mid + near), mid)
            top = mid.astype(BF16).astype(F32)
            stack += [top, mid - top]
        stack = jnp.concatenate(stack, 0)
        low_stack = iota(stack.shape, 1) < 64
        stack = jnp.concatenate(
            [
                jnp.where(low_stack, stack, 0.0),
                jnp.where(low_stack, 0.0, stack),
                jnp.zeros((64, 128), F32),
            ],
            0,
        )
        spans.append(dot(take, stack.astype(BF16), NT).astype(BF16))

    for b in range(2):

        @pl.when(has_y[b])
        def _(b=b):
            pltpu.make_async_remote_copy(
                src_ref=row_ref.at[b],
                dst_ref=row_in_ref.at[b],
                send_sem=row_send.at[b],
                recv_sem=row_recv.at[b],
                device_id={"gy": gy + 2 * b - 1},
                device_id_type=MESH,
            ).wait()
            rows = y_rows(b * (height - 1))
            merged_ref[rows] = 0.5 * (merged_ref[rows] + row_in_ref[b])

    for d in range(1, across):
        came = lax.rem(gx - d + across, across)
        pltpu.make_async_remote_copy(
            src_ref=table_ref.at[gx],
            dst_ref=table_ref.at[came],
            send_sem=panel_send.at[d - 1],
            recv_sem=panel_recv.at[d - 1],
            device_id={"gx": lax.rem(gx + d, across)},
            device_id_type=MESH,
        ).wait()

    loads[6].wait()
    table = jnp.concatenate([table_ref[:, c].reshape(spots, 128) for c in range(3)], 1)
    high, low = halves(table)
    incoming = dot(jnp.concatenate([gather, gather], 1), jnp.concatenate([high, low], 0))
    lane_two = iota((2 * pairs, 128), 1) >> 6
    for c in range(3):
        part = incoming[:, c * 128 : c * 128 + 128]
        part = jnp.where(lane_two == source_half, part, pltpu.roll(part, 64, 1))
        first, second = part[:pairs], part[pairs:]
        spaced = []
        for p in range(blocks // 2):
            block_id = lane_half + 2 * p
            spaced.append(
                jnp.where(chosen[0] == block_id, first, 0.0)
                + jnp.where(chosen[1] == block_id, second, 0.0)
            )
        high, low = halves(jnp.concatenate(spaced, 1))
        packed_in = jnp.concatenate([high, low, high], 1)
        packed_in = jnp.concatenate([packed_in, packed_in], 0)
        projected = dot(weight_ref[...], packed_in, NT)
        top = projected.astype(BF16).astype(F32)
        projected = jnp.where(iota((64, 2 * pairs), 1) < pairs, top, projected - top).astype(BF16)
        change = dot(jnp.concatenate([projected, spans[c]], 1), spread_ref[...])
        for k in range(layers):
            stack = merged_ref[pl.ds((c * depth + 8 * k) * height, plane), :]
            stack = stack.reshape(8, height, width)
            for j in range(tall):
                at = (k * tall + j) * width
                value = stack[:, 8 * j : 8 * j + 8].reshape(64, width) * factor[:, at : at + width]
                value = time_step * (value + change[:, at : at + width])
                spot = (c, pl.ds(8 * k, 8), pl.ds(8 * j, 8))
                value = 2.0 / 3.0 * (sec_ref[spot] + value.reshape(8, 8, width))
                out_ref[spot] = start_ref[spot] * (1.0 / 3.0) + value


def local(initial, sectioned, rotor_faces, intersections, live_counts, mortar_blocks):
    across = lax.axis_size("gx")
    along = lax.axis_size("gy")
    _, depth, height, width = sectioned.shape
    left, right = operators(height, width)
    plane = 8 * height
    columns = (depth // 8) * (height // 8) * width
    group = 2 if (depth // 8) % 2 == 0 else 1
    packed = rotor_faces.shape[1] // 2
    pairs = intersections.shape[1] // 2
    blocks = mortar_blocks.shape[0]
    staged = pl.pallas_call(
        functools.partial(step_kernel, across, along),
        out_shape=pltpu.VMEM(sectioned.shape, F32),
        in_specs=[pl.BlockSpec(memory_space=pltpu.HBM)] * 8,
        out_specs=pl.BlockSpec(memory_space=pltpu.VMEM),
        scratch_shapes=[
            pltpu.VMEM(initial.shape, F32),
            pltpu.VMEM(sectioned.shape, F32),
            pltpu.VMEM(rotor_faces.shape, jnp.int32),
            pltpu.VMEM((3, 1, 2 * pairs), jnp.int32),
            pltpu.VMEM((1, 1), jnp.int32),
            pltpu.VMEM(mortar_blocks.shape, F32),
            pltpu.VMEM(left.shape, BF16),
            pltpu.VMEM(right.shape, BF16),
            pltpu.SemaphoreType.DMA((7,)),
            pltpu.SemaphoreType.DMA((depth // 8 // group,)),
            pltpu.VMEM((3, 3 * plane, group * width), F32),
            pltpu.VMEM((3, group * plane, 2 * width), F32),
            pltpu.VMEM((3 * depth * height, width), F32),
            pltpu.VMEM((3 * depth * height, width), F32),
            pltpu.VMEM((across, 3, packed, 128), F32),
            pltpu.VMEM((2, 3, 8, 128), F32),
            pltpu.VMEM((2, 3, 3, 8, 128), F32),
            pltpu.VMEM((2, 3 * depth, width), F32),
            pltpu.VMEM((2, 3 * depth, width), F32),
            pltpu.VMEM((64, 3 * 64 * blocks), BF16),
            pltpu.VMEM((2 * pairs + 128, columns), BF16),
            pltpu.SemaphoreType.DMA((across - 1,)),
            pltpu.SemaphoreType.DMA((across - 1,)),
            pltpu.SemaphoreType.DMA((2, 3)),
            pltpu.SemaphoreType.DMA((2, 3)),
            pltpu.SemaphoreType.DMA((2,)),
            pltpu.SemaphoreType.DMA((2,)),
        ],
        compiler_params=pltpu.CompilerParams(
            collective_id=0, has_side_effects=True, vmem_limit_bytes=67043328 - 4 * int(np.prod(sectioned.shape))
        ),
        name="step",
    )(
        sectioned,
        rotor_faces,
        jnp.transpose(intersections, (2, 0, 1)),
        live_counts,
        mortar_blocks,
        jnp.asarray(left),
        jnp.asarray(right),
        initial,
    )
    return pl.pallas_call(
        store_kernel,
        out_shape=jax.ShapeDtypeStruct(sectioned.shape, F32),
        in_specs=[pl.BlockSpec(memory_space=pltpu.VMEM)],
        out_specs=pl.BlockSpec(memory_space=pltpu.HBM),
        scratch_shapes=[pltpu.SemaphoreType.DMA((3,))],
        compiler_params=pltpu.CompilerParams(vmem_limit_bytes=4*1024*1024),
        name="store",
    )(staged)


def store_kernel(x_ref, out_hbm, sem):
    for c in range(3):
        pltpu.make_async_copy(x_ref.at[c], out_hbm.at[c], sem.at[c]).start()
    for c in range(3):
        pltpu.make_async_copy(x_ref.at[c], out_hbm.at[c], sem.at[c]).wait()


def solution(mesh):
    return jax.shard_map(
        local,
        mesh=mesh,
        in_specs=(
            P(None, None, "gy", "gx"),
            P(None, None, "gy", "gx"),
            P("gy", "gx"),
            P("gy", "gx", None),
            P("gy", "gx"),
            P(),
        ),
        out_specs=P(None, None, "gy", "gx"),
        check_vma=False,
    )
```

```python
import functools

import jax
import jax.numpy as jnp
import numpy as np
from jax import lax
from jax.experimental import pallas as pl
from jax.experimental.pallas import tpu as pltpu
from jax.sharding import PartitionSpec as P

time_step = 0.02
viscosity = 0.005
smagorinsky = 0.002
gll_interior = [
    -0.8717401485096066,
    -0.5917001814331423,
    -0.2092992179024789,
    0.2092992179024789,
    0.5917001814331423,
    0.8717401485096066,
]


def legendre_seven(points):
    lower_poly = points * 0.0 + 1.0
    current = points * 1.0
    for order_at in range(1, 7):
        following = ((2 * order_at + 1) * points * current - order_at * lower_poly) / (order_at + 1)
        lower_poly = current
        current = following
    return current


def gll_tables():
    degree = 7
    points = np.array([-1.0] + gll_interior + [1.0])
    values = legendre_seven(points)
    slope_table = np.zeros((degree + 1, degree + 1))
    for row_at in range(degree + 1):
        for col_at in range(degree + 1):
            if row_at != col_at:
                slope_table[row_at, col_at] = values[row_at] / (
                    values[col_at] * (points[row_at] - points[col_at])
                )
    slope_table[0, 0] = -degree * (degree + 1) / 4.0
    slope_table[degree, degree] = degree * (degree + 1) / 4.0
    return (slope_table, slope_table @ slope_table)


F32 = jnp.float32
BF16 = jnp.bfloat16
MESH = pl.DeviceIdType.MESH
NT = (((1,), (1,)), ((), ()))
NN = (((1,), (0,)), ((), ()))


def split_table(table):
    table = np.asarray(table, np.float32)
    high = table.astype(BF16)
    return high, (table - high.astype(np.float32)).astype(BF16)


def operators(height, width):
    slope, curve = gll_tables()
    tall = np.eye(height // 8)
    eye = np.eye(8)
    left = np.concatenate(
        [
            np.kron(tall, np.kron(eye, slope)),
            np.kron(tall, np.kron(slope, eye)),
            np.kron(tall, np.kron(eye, curve) + np.kron(curve, eye)),
        ]
    )
    high, low = split_table(left)
    left = np.concatenate([high, high, low], 1)
    cols = np.eye(width // 8)
    along, twice = np.kron(cols, slope), np.kron(cols, curve)
    high, low = split_table(np.concatenate([along.T, twice.T], 1))
    right = np.concatenate([high, high, low], 0)
    rows = face_rows(width)
    nodes = list(range(0, width, 8)) + [width - 1]
    face = np.zeros((-(-3 * rows // 16) * 16, width))
    for at, table in enumerate([np.eye(width), along, twice]):
        face[at * rows : at * rows + len(nodes)] = table[nodes]
    high, low = split_table(face)
    face = np.concatenate([high, high, low], 1)
    return left, right, face


def face_rows(width):
    return -(-(width // 8 + 1) // 8) * 8


def halves(value):
    high = value.astype(BF16)
    return high, (value - high.astype(F32)).astype(BF16)


def dot(left, right, dims=NN):
    return lax.dot_general(left, right, dims, preferred_element_type=F32)


def iota(shape, dim):
    return lax.broadcasted_iota(jnp.int32, shape, dim)


def split_index(value, size):
    if size & (size - 1) == 0:
        return value >> (size.bit_length() - 1), value & (size - 1)
    return value // size, value % size


def rate_of(vel, grad, lap):
    strain = grad[0][0] * grad[0][0] + grad[1][1] * grad[1][1] + grad[2][2] * grad[2][2]
    for one, two in ((0, 1), (0, 2), (1, 2)):
        both = grad[one][two] + grad[two][one]
        strain = strain + 0.5 * (both * both)
    eddy = viscosity + smagorinsky * jnp.sqrt(2.0 * strain + 1e-06)
    return [
        eddy * lap[c] - (vel[0] * grad[0][c] + vel[1] * grad[1][c] + vel[2] * grad[2][c])
        for c in range(3)
    ]


def step_kernel(
    across,
    along,
    sec_hbm,
    rotor_hbm,
    entry_hbm,
    count_hbm,
    mortar_hbm,
    left_hbm,
    right_hbm,
    face_hbm,
    start_hbm,
    table_ref,
    pre_ref,
    weight_ref,
    spread_ref,
    span_ref,
    gather_ref,
    half_ref,
    chosen_ref,
    start_ref,
    sec_ref,
    rotor_ref,
    entry_ref,
    count_ref,
    mortar_ref,
    left_ref,
    right_ref,
    face_ref,
    load_sem,
    sec_sem,
    split_ref,
    small_ref,
    side_ref,
    rate_ref,
    yz_ref,
    x_ref,
    merged_ref,
    edge_ref,
    edge_in_ref,
    row_ref,
    row_in_ref,
    panel_send,
    panel_recv,
    edge_send,
    edge_recv,
    row_send,
    row_recv,
):
    _, depth, height, width = sec_ref.shape
    layers, tall = depth // 8, height // 8
    plane = 8 * height
    columns = layers * tall * width
    slots = rotor_ref.shape[1]
    packed = slots // 2
    shift = packed.bit_length() - 1
    entries = entry_ref.shape[2]
    pairs = entries // 2
    blocks = mortar_ref.shape[0]
    lanes_x = width // 8
    rows = face_rows(width)
    gx = lax.axis_index("gx")
    gy = lax.axis_index("gy")
    has_x = (gx > 0, gx < across - 1)
    has_y = (gy > 0, gy < along - 1)

    def number(flag):
        return jnp.where(flag, 1, 0)

    group = 2 if layers % 2 == 0 else 1
    groups = layers // group
    scale = 2.0 / 3.0 * time_step

    def sec_load(at):
        span = pl.ds(pl.multiple_of(at * group * 8, 8), group * 8)
        return pltpu.make_async_copy(sec_hbm.at[:, span], sec_ref.at[:, span], sec_sem.at[at])

    loads = [
        pltpu.make_async_copy(source, target, load_sem.at[i])
        for i, (source, target) in enumerate(
            [
                (face_hbm, face_ref),
                (left_hbm, left_ref),
                (rotor_hbm, rotor_ref),
                (right_hbm, right_ref),
                (entry_hbm, entry_ref),
                (count_hbm, count_ref),
                (mortar_hbm, mortar_ref),
                (start_hbm, start_ref),
            ]
        )
    ]
    loads[0].start()
    for at in range(groups):
        sec_load(at).start()
    for load in loads[1:]:
        load.start()

    barrier = pltpu.get_barrier_semaphore()
    for d in range(1, across):
        pl.semaphore_signal(
            barrier, inc=1, device_id={"gx": lax.rem(gx + d, across)}, device_id_type=MESH
        )
    for b in range(2):
        for dx in (-1, 0, 1):
            there = has_y[b] if dx == 0 else has_y[b] & has_x[(dx + 1) // 2]

            @pl.when(there)
            def _(b=b, dx=dx):
                pl.semaphore_signal(
                    barrier,
                    inc=1,
                    device_id={"gx": gx + dx, "gy": gy + 2 * b - 1},
                    device_id_type=MESH,
                )

    loads[0].wait()
    for at in range(groups):
        sec_load(at).wait()
        for c in range(3):
            both = []
            for q in range(group):
                stack = sec_ref[c, pl.ds((at * group + q) * 8, 8)]
                value = jnp.concatenate(
                    [stack[:, 8 * j : 8 * j + 8].reshape(64, width) for j in range(tall)], 0
                )
                high, low = halves(value)
                split_ref[c, at * group + q, :, pl.ds(0, width)] = high
                split_ref[c, at * group + q, :, pl.ds(width, width)] = low
                both.append(jnp.concatenate([high, low, high], 1))
            small_ref[c, at] = dot(face_ref[...], jnp.concatenate(both, 0), NT)
    loads[1].wait()
    values = jnp.concatenate(
        [
            small_ref[c, k // group, pl.ds(0, rows), pl.ds(k % group * plane, plane)]
            for k in range(layers)
            for c in range(3)
        ],
        0,
    )
    high, low = halves(values)
    side_ref[...] = dot(jnp.concatenate([high, low, high], 1), left_ref[...], NT)
    for k in range(layers):
        vel, grad, lap = [], [[], [], []], []
        for c in range(3):
            lanes = pl.ds(k % group * plane, plane)
            own_rows = pl.ds((k * 3 + c) * rows, rows)
            vel.append(small_ref[c, k // group, pl.ds(0, rows), lanes])
            grad[0].append(small_ref[c, k // group, pl.ds(rows, rows), lanes])
            grad[1].append(side_ref[own_rows, pl.ds(0, plane)])
            grad[2].append(side_ref[own_rows, pl.ds(plane, plane)])
            lap.append(
                small_ref[c, k // group, pl.ds(2 * rows, rows), lanes]
                + side_ref[own_rows, pl.ds(2 * plane, plane)]
            )
        for c, rate in enumerate(rate_of(vel, grad, lap)):
            rate_ref[pl.ds((c * layers + k) * rows, rows), :] = rate

    loads[2].wait()
    square = iota((slots, slots), 0) == iota((slots, slots), 1)
    faces = jnp.broadcast_to(rotor_ref[...].astype(F32), (slots, slots))
    faces = jnp.sum(jnp.where(square, faces, 0.0), axis=1, keepdims=True).astype(jnp.int32)
    rest, face_x = split_index(faces, lanes_x)
    face_z, face_y = split_index(rest, tall)
    line = layers * rows
    pick = jnp.where(iota((slots, line), 1) == face_z * rows + face_x, 1.0, 0.0).astype(BF16)
    parts = []
    for c in range(3):
        high, low = halves(rate_ref[pl.ds(c * line, line), :])
        parts.append(jnp.concatenate([high, low], 0))
    found = dot(jnp.concatenate([pick, pick], 1), jnp.concatenate(parts, 1))
    own_half = iota((slots, plane), 1) >> 6 == face_y
    for c in range(3):
        value = jnp.where(own_half, found[:, c * plane : c * plane + plane], 0.0)
        value = value + pltpu.roll(value, 64, 1)
        table_ref[gx, c] = jnp.where(
            iota((packed, plane), 1) < 64, value[:packed], value[packed:]
        )
        for a in range(2):
            edge_ref[a, c] = jnp.zeros(edge_ref.shape[2:], F32)
            edge_ref[a, c, pl.ds(0, layers)] = rate_ref[
                pl.ds(c * line + a * lanes_x, layers, stride=rows), :
            ]

    expected = across - 1
    for b in range(2):
        expected = expected + number(has_y[b]) * (1 + number(has_x[0]) + number(has_x[1]))
    pl.semaphore_wait(barrier, expected)

    def edge_copy(a, dy):
        return pltpu.make_async_remote_copy(
            src_ref=edge_ref.at[a],
            dst_ref=edge_in_ref.at[1 - a, 1 - dy],
            send_sem=edge_send.at[a, dy + 1],
            recv_sem=edge_recv.at[1 - a, 1 - dy],
            device_id={"gx": gx + 2 * a - 1, "gy": gy + dy},
            device_id_type=MESH,
        )

    def edge_there(a, dy):
        return has_x[a] if dy == 0 else has_x[a] & has_y[(dy + 1) // 2]

    for d in range(1, across):
        pltpu.make_async_remote_copy(
            src_ref=table_ref.at[gx],
            dst_ref=table_ref.at[gx],
            send_sem=panel_send.at[d - 1],
            recv_sem=panel_recv.at[d - 1],
            device_id={"gx": lax.rem(gx + d, across)},
            device_id_type=MESH,
        ).start()

    edge_list = [(a, dy) for a in range(2) for dy in (-1, 0, 1)]
    for a, dy in edge_list:

        @pl.when(edge_there(a, dy))
        def _(a=a, dy=dy):
            edge_copy(a, dy).start()

        @pl.when(jnp.logical_not(edge_there(a, dy)))
        def _(a=a, dy=dy):
            edge_in_ref[a, dy + 1] = jnp.zeros(edge_in_ref.shape[2:], F32)

    lane = iota((8, width), 1)
    y_at = iota((8, width), 0)
    y8 = lane & 7
    own = jnp.where((y8 == 0) | (y8 == 7), 0.5, 1.0)
    own = jnp.where((lane == 0) & jnp.logical_not(has_x[0]), 1.0, own)
    own = jnp.where((lane == width - 1) & jnp.logical_not(has_x[1]), 1.0, own)
    other = jnp.where(((y8 == 0) & (lane > 0)) | ((y8 == 7) & (lane < width - 1)), 0.5, 0.0)
    loads[3].wait()

    def row_copy(b, at):
        return pltpu.make_async_remote_copy(
            src_ref=row_ref.at[b, at],
            dst_ref=row_in_ref.at[1 - b, at],
            send_sem=row_send.at[b, at],
            recv_sem=row_recv.at[1 - b, at],
            device_id={"gy": gy + 2 * b - 1},
            device_id_type=MESH,
        )

    def layer_group(at, carry):
        for c in range(3):
            pieces = [split_ref[c, at * group + q] for q in range(group)]
            wide = jnp.concatenate(pieces, 0)
            high, low = wide[:, :width], wide[:, width:]
            x_ref[c] = dot(jnp.concatenate([high, low, high], 1), right_ref[...])
            high = jnp.concatenate([piece[:, :width] for piece in pieces], 1)
            low = jnp.concatenate([piece[:, width:] for piece in pieces], 1)
            yz_ref[c] = dot(left_ref[...], jnp.concatenate([high, low, high], 0))
        for q in range(group):
            lanes = pl.ds(q * width, width)
            for z in range(8):
                z_at = (at * group + q) * 8 + z
                found = []
                for j in range(tall):
                    spot = j * 64 + 8 * z
                    x_rows = pl.ds(q * plane + spot, 8)
                    vel = [sec_ref[c, z_at, pl.ds(8 * j, 8)] for c in range(3)]
                    grad, lap = [[], [], []], []
                    for c in range(3):
                        grad[0].append(x_ref[c, x_rows, pl.ds(0, width)])
                        grad[1].append(yz_ref[c, pl.ds(spot, 8), lanes])
                        grad[2].append(yz_ref[c, pl.ds(plane + spot, 8), lanes])
                        lap.append(
                            x_ref[c, x_rows, pl.ds(width, width)]
                            + yz_ref[c, pl.ds(2 * plane + spot, 8), lanes]
                        )
                    merged = []
                    for rate in rate_of(vel, grad, lap):
                        partner = jnp.where(
                            y8 == 0, pltpu.roll(rate, 1, 1), pltpu.roll(rate, width - 1, 1)
                        )
                        merged.append(own * rate + other * partner)
                    found.append(merged)
                for c in range(3):
                    at_row = pl.multiple_of((c * depth + z_at) * height, height)
                    row_ref[0, at, c, pl.ds(q * 8 + z, 1)] = found[0][c][0:1]
                    row_ref[1, at, c, pl.ds(q * 8 + z, 1)] = found[tall - 1][c][7:8]
                    for j in range(tall):
                        value = found[j][c]
                        if j > 0:
                            mean = 0.5 * (value + pltpu.roll(found[j - 1][c], 1, 0))
                            value = jnp.where(y_at == 0, mean, value)
                        if j < tall - 1:
                            mean = 0.5 * (value + pltpu.roll(found[j + 1][c], 7, 0))
                            value = jnp.where(y_at == 7, mean, value)
                        merged_ref[pl.ds(at_row + 8 * j, 8), :] = value
        for b in range(2):

            @pl.when(has_y[b])
            def _(b=b):
                row_copy(b, at).start()

        return carry

    lax.fori_loop(0, groups, layer_group, 0)

    for load in loads[4:]:
        load.wait()

    for c in range(3):
        for k in range(1, layers):
            top = pl.ds((c * depth + 8 * k - 1) * height, height)
            bottom = pl.ds((c * depth + 8 * k) * height, height)
            mean = 0.5 * (merged_ref[top, :] + merged_ref[bottom, :])
            merged_ref[top, :] = mean
            merged_ref[bottom, :] = mean

    entry_lane = iota((pairs, entries), 1)
    entry_row = 2 * iota((pairs, entries), 0)

    def upright(kind, odd_one):
        values = jnp.broadcast_to(entry_ref[kind].astype(F32), (pairs, entries))
        values = jnp.where(entry_lane == entry_row + odd_one, values, 0.0)
        return jnp.sum(values, axis=1, keepdims=True).astype(jnp.int32)

    live = 2 * iota((pairs, 1), 0) < count_ref[...]
    stator = jnp.where(live, 8 * upright(0, 0), -1)
    spread = jnp.where(iota((pairs, columns), 1) == stator, 0.5, 0.0)
    factor = 1.0 - jnp.max(spread, axis=0, keepdims=True)
    spread_ref[pl.ds(0, pairs), :] = spread.astype(BF16)
    spread_ref[pl.ds(pairs, pairs), :] = spread.astype(BF16)
    row_e = iota((128, 1), 0)
    layer_e = row_e & 7
    side_e = (row_e >> 4) & 1
    tall_e = row_e >> 5
    kept = (tall_e < tall) & (layer_e < layers)
    kept = kept & (jnp.where(side_e == 0, number(has_x[0]), number(has_x[1])) > 0)
    to_e = jnp.where(kept, (layer_e * tall + tall_e) * width + side_e * (width - 1), -1)
    spread_ref[pl.ds(2 * pairs, 128), :] = jnp.where(
        iota((128, columns), 1) == to_e, 0.5 * factor, 0.0
    ).astype(BF16)

    for k in range(layers):
        for j in range(tall):
            at = (k * tall + j) * width
            keep = jnp.broadcast_to(scale * factor[:, at : at + width], (8, width))
            if j == 0:
                keep = jnp.where((y_at == 0) & has_y[0], 0.5 * keep, keep)
            if j == tall - 1:
                keep = jnp.where((y_at == 7) & has_y[1], 0.5 * keep, keep)
            for c in range(3):
                for z in range(8 * k, 8 * k + 8):
                    spot = pl.ds((c * depth + z) * height + 8 * j, 8)
                    pre_ref[spot, :] = (
                        start_ref[c, z, pl.ds(8 * j, 8)] * (1.0 / 3.0)
                        + sec_ref[c, z, pl.ds(8 * j, 8)] * (2.0 / 3.0)
                        + merged_ref[spot, :] * keep
                    )

    depth_k = blocks * 64
    for p in range(blocks // 2):
        high, low = halves(
            scale * jnp.concatenate([mortar_ref[2 * p], mortar_ref[2 * p + 1]], 1)
        )
        weight_ref[:, pl.ds(p * 128, 128)] = high
        weight_ref[:, pl.ds(depth_k + p * 128, 128)] = high
        weight_ref[:, pl.ds(2 * depth_k + p * 128, 128)] = low

    lane_half = iota((pairs, 128), 1) >> 6
    for odd_one in (0, 1):
        chosen = jnp.where(live, upright(2, odd_one), -1)
        for p in range(blocks // 2):
            chosen_ref[pl.ds(odd_one * pairs, pairs), pl.ds(p * 128, 128)] = jnp.where(
                chosen == lane_half + 2 * p, 1.0, 0.0
            ).astype(BF16)
    source = jnp.concatenate([upright(1, 0), upright(1, 1)], 0)
    spots = across * packed
    table_row = iota((2 * pairs, spots), 1)
    first_id = table_row + ((table_row >> shift) << shift)
    gather = jnp.where((source == first_id) | (source == first_id + packed), 1.0, 0.0).astype(BF16)
    gather_ref[:, pl.ds(0, spots)] = gather
    gather_ref[:, pl.ds(spots, spots)] = gather
    source_half = (source >> shift) & 1
    half_ref[...] = jnp.where(iota((2 * pairs, 128), 1) >> 6 == source_half, 1, 0)
    take = jnp.where((iota((64, 128), 1) & 63) == iota((64, 128), 0), 1.0, 0.0).astype(BF16)

    e_lane = iota((8, 128), 1)
    e_row = iota((8, 128), 0)
    e_y = e_lane & 7
    e_z = (e_lane >> 3) & 7
    e_low = e_lane < 64
    for a, dy in edge_list:

        @pl.when(edge_there(a, dy))
        def _(a=a, dy=dy):
            pltpu.make_async_remote_copy(
                src_ref=edge_ref.at[a],
                dst_ref=edge_in_ref.at[a, dy + 1],
                send_sem=edge_send.at[a, dy + 1],
                recv_sem=edge_recv.at[a, dy + 1],
                device_id={"gx": gx + 2 * a - 1, "gy": gy + dy},
                device_id_type=MESH,
            ).wait()

    y_move = ((e_y == 0) & (jnp.logical_not(e_low) | has_y[0])) | (
        (e_y == 7) & (e_low | has_y[1])
    )
    z_move = ((e_z == 0) & (e_row > 0)) | ((e_z == 7) & (e_row < layers - 1))
    for c in range(3):
        stack = []
        for a in range(2):
            mid = edge_in_ref[a, 1, c]
            near = jnp.where(
                e_y == 0,
                jnp.where(e_low, pltpu.roll(edge_in_ref[a, 0, c], 57, 1), pltpu.roll(mid, 57, 1)),
                jnp.where(e_low, pltpu.roll(mid, 71, 1), pltpu.roll(edge_in_ref[a, 2, c], 71, 1)),
            )
            mid = jnp.where(y_move, 0.5 * (mid + near), mid)
            near = jnp.where(
                e_z == 0,
                pltpu.roll(pltpu.roll(mid, 72, 1), 1, 0),
                pltpu.roll(pltpu.roll(mid, 56, 1), 7, 0),
            )
            mid = scale * jnp.where(z_move, 0.5 * (mid + near), mid)
            top = mid.astype(BF16).astype(F32)
            stack += [top, mid - top]
        stack = jnp.concatenate(stack, 0)
        low_stack = iota(stack.shape, 1) < 64
        stack = jnp.concatenate(
            [
                jnp.where(low_stack, stack, 0.0),
                jnp.where(low_stack, 0.0, stack),
                jnp.zeros((64, 128), F32),
            ],
            0,
        )
        span_ref[pl.ds(64 * c, 64), :] = dot(take, stack.astype(BF16), NT).astype(BF16)

    z_at = iota((depth, width), 0)
    z8 = z_at & 7
    z_low = (z8 == 0) & (z_at > 0)
    z_high = (z8 == 7) & (z_at < depth - 1)
    for b in range(2):

        @pl.when(has_y[b])
        def _(b=b):
            for at in range(groups):
                pltpu.make_async_remote_copy(
                    src_ref=row_ref.at[b, at],
                    dst_ref=row_in_ref.at[b, at],
                    send_sem=row_send.at[b, at],
                    recv_sem=row_recv.at[b, at],
                    device_id={"gy": gy + 2 * b - 1},
                    device_id_type=MESH,
                ).wait()
            j = b * (tall - 1)
            keep = jnp.concatenate(
                [
                    jnp.broadcast_to(
                        0.5 * scale * factor[:, (k * tall + j) * width : (k * tall + j + 1) * width],
                        (8, width),
                    )
                    for k in range(layers)
                ],
                0,
            )
            for c in range(3):
                value = jnp.concatenate([row_in_ref[b, at, c] for at in range(groups)], 0)
                near = jnp.where(
                    z_low, pltpu.roll(value, 1, 0), pltpu.roll(value, depth - 1, 0)
                )
                value = jnp.where(z_low | z_high, 0.5 * (value + near), value)
                spot = (pl.ds(c * depth * height + b * (height - 1), depth, stride=height), slice(None))
                pre_ref[spot] = pre_ref[spot] + keep * value

    for d in range(1, across):
        came = lax.rem(gx - d + across, across)
        pltpu.make_async_remote_copy(
            src_ref=table_ref.at[gx],
            dst_ref=table_ref.at[came],
            send_sem=panel_send.at[d - 1],
            recv_sem=panel_recv.at[d - 1],
            device_id={"gx": lax.rem(gx + d, across)},
            device_id_type=MESH,
        ).wait()


def finish_kernel(
    table_ref,
    pre_ref,
    weight_ref,
    spread_ref,
    span_ref,
    gather_ref,
    half_ref,
    chosen_ref,
    out_hbm,
    out_ref,
    out_sem,
):
    _, depth, height, width = out_ref.shape
    layers, tall = depth // 8, height // 8
    across, _, packed, _ = table_ref.shape
    spots = across * packed
    copies = chosen_ref.shape[1] // 128
    table = jnp.concatenate([table_ref[:, c].reshape(spots, 128) for c in range(3)], 1)
    high, low = halves(table)
    incoming = dot(gather_ref[...], jnp.concatenate([high, low], 0))
    straight = half_ref[...] > 0
    chosen = chosen_ref[...]
    lefts = []
    for c in range(3):
        part = incoming[:, c * 128 : c * 128 + 128]
        high, low = halves(jnp.where(straight, part, pltpu.roll(part, 64, 1)))
        high = jnp.concatenate([high] * copies, 1) * chosen
        low = jnp.concatenate([low] * copies, 1) * chosen
        projected = dot(weight_ref[...], jnp.concatenate([high, low, high], 1), NT)
        projected = projected + pltpu.roll(projected, projected.shape[1] // 2, 1)
        top = projected.astype(BF16).astype(F32)
        first = iota(projected.shape, 1) < projected.shape[1] // 2
        projected = jnp.where(first, top, projected - top).astype(BF16)
        lefts.append(jnp.concatenate([projected, span_ref[pl.ds(64 * c, 64), :]], 1))
    lefts = jnp.concatenate(lefts, 0)
    stores = []
    for k in range(layers):
        change = dot(lefts, spread_ref[:, pl.ds(k * tall * width, tall * width)])
        for c in range(3):
            for j in range(tall):
                for z in range(8):
                    row = 64 * c + 8 * z
                    out_ref[c, 8 * k + z, pl.ds(8 * j, 8)] = (
                        pre_ref[pl.ds((c * depth + 8 * k + z) * height + 8 * j, 8), :]
                        + change[row : row + 8, j * width : j * width + width]
                    )
        span = pl.ds(8 * k, 8)
        stores.append(
            pltpu.make_async_copy(out_ref.at[:, span], out_hbm.at[:, span], out_sem.at[k])
        )
        stores[-1].start()
    for store in stores:
        store.wait()


def local(initial, sectioned, rotor_faces, intersections, live_counts, mortar_blocks):
    across = lax.axis_size("gx")
    along = lax.axis_size("gy")
    _, depth, height, width = sectioned.shape
    left, right, face = operators(height, width)
    plane = 8 * height
    layers = depth // 8
    columns = layers * (height // 8) * width
    group = 2 if layers % 2 == 0 else 1
    groups = layers // group
    packed = rotor_faces.shape[1] // 2
    pairs = intersections.shape[1] // 2
    blocks = mortar_blocks.shape[0]
    rows = face_rows(width)
    passed = [
        ((across, 3, packed, 128), F32),
        ((3 * depth * height, width), F32),
        ((64, 3 * 64 * blocks), BF16),
        ((2 * pairs + 128, columns), BF16),
        ((3 * 64, 128), BF16),
        ((2 * pairs, 2 * across * packed), BF16),
        ((2 * pairs, 128), jnp.int32),
        ((2 * pairs, 64 * blocks), BF16),
    ]
    room = sum(int(np.prod(shape)) * jnp.dtype(kind).itemsize for shape, kind in passed)
    staged = pl.pallas_call(
        functools.partial(step_kernel, across, along),
        out_shape=[pltpu.VMEM(shape, kind) for shape, kind in passed],
        in_specs=[pl.BlockSpec(memory_space=pltpu.HBM)] * 9,
        out_specs=[pl.BlockSpec(memory_space=pltpu.VMEM)] * len(passed),
        scratch_shapes=[
            pltpu.VMEM(initial.shape, F32),
            pltpu.VMEM(sectioned.shape, F32),
            pltpu.VMEM(rotor_faces.shape, jnp.int32),
            pltpu.VMEM((3, 1, 2 * pairs), jnp.int32),
            pltpu.VMEM((1, 1), jnp.int32),
            pltpu.VMEM(mortar_blocks.shape, F32),
            pltpu.VMEM(left.shape, BF16),
            pltpu.VMEM(right.shape, BF16),
            pltpu.VMEM(face.shape, BF16),
            pltpu.SemaphoreType.DMA((8,)),
            pltpu.SemaphoreType.DMA((groups,)),
            pltpu.VMEM((3, layers, plane, 2 * width), BF16),
            pltpu.VMEM((3, groups, face.shape[0], group * plane), F32),
            pltpu.VMEM((3 * layers * rows, 3 * plane), F32),
            pltpu.VMEM((3 * layers * rows, plane), F32),
            pltpu.VMEM((3, 3 * plane, group * width), F32),
            pltpu.VMEM((3, group * plane, 2 * width), F32),
            pltpu.VMEM((3 * depth * height, width), F32),
            pltpu.VMEM((2, 3, 8, 128), F32),
            pltpu.VMEM((2, 3, 3, 8, 128), F32),
            pltpu.VMEM((2, groups, 3, group * 8, width), F32),
            pltpu.VMEM((2, groups, 3, group * 8, width), F32),
            pltpu.SemaphoreType.DMA((across - 1,)),
            pltpu.SemaphoreType.DMA((across - 1,)),
            pltpu.SemaphoreType.DMA((2, 3)),
            pltpu.SemaphoreType.DMA((2, 3)),
            pltpu.SemaphoreType.DMA((2, groups)),
            pltpu.SemaphoreType.DMA((2, groups)),
        ],
        compiler_params=pltpu.CompilerParams(
            collective_id=0, has_side_effects=True, vmem_limit_bytes=67043328 - room
        ),
        name="step",
    )(
        sectioned,
        rotor_faces,
        jnp.transpose(intersections, (2, 0, 1)),
        live_counts,
        mortar_blocks,
        jnp.asarray(left),
        jnp.asarray(right),
        jnp.asarray(face),
        initial,
    )
    return pl.pallas_call(
        finish_kernel,
        out_shape=jax.ShapeDtypeStruct(sectioned.shape, F32),
        in_specs=[pl.BlockSpec(memory_space=pltpu.VMEM)] * len(passed),
        out_specs=pl.BlockSpec(memory_space=pltpu.HBM),
        scratch_shapes=[pltpu.VMEM(sectioned.shape, F32), pltpu.SemaphoreType.DMA((layers,))],
        compiler_params=pltpu.CompilerParams(vmem_limit_bytes=32 * 1024 * 1024),
        name="finish",
    )(*staged)


def solution(mesh):
    return jax.shard_map(
        local,
        mesh=mesh,
        in_specs=(
            P(None, None, "gy", "gx"),
            P(None, None, "gy", "gx"),
            P("gy", "gx"),
            P("gy", "gx", None),
            P("gy", "gx"),
            P(),
        ),
        out_specs=P(None, None, "gy", "gx"),
        check_vma=False,
    )
```

```python
import functools

import jax
import jax.numpy as jnp
import numpy as np
from jax import lax
from jax.experimental import pallas as pl
from jax.experimental.pallas import tpu as pltpu
from jax.sharding import PartitionSpec as P

time_step = 0.02
viscosity = 0.005
smagorinsky = 0.002
gll_interior = [
    -0.8717401485096066,
    -0.5917001814331423,
    -0.2092992179024789,
    0.2092992179024789,
    0.5917001814331423,
    0.8717401485096066,
]


def legendre_seven(points):
    lower_poly = points * 0.0 + 1.0
    current = points * 1.0
    for order_at in range(1, 7):
        following = ((2 * order_at + 1) * points * current - order_at * lower_poly) / (order_at + 1)
        lower_poly = current
        current = following
    return current


def gll_tables():
    degree = 7
    points = np.array([-1.0] + gll_interior + [1.0])
    values = legendre_seven(points)
    slope_table = np.zeros((degree + 1, degree + 1))
    for row_at in range(degree + 1):
        for col_at in range(degree + 1):
            if row_at != col_at:
                slope_table[row_at, col_at] = values[row_at] / (
                    values[col_at] * (points[row_at] - points[col_at])
                )
    slope_table[0, 0] = -degree * (degree + 1) / 4.0
    slope_table[degree, degree] = degree * (degree + 1) / 4.0
    return (slope_table, slope_table @ slope_table)


F32 = jnp.float32
BF16 = jnp.bfloat16
MESH = pl.DeviceIdType.MESH
NT = (((1,), (1,)), ((), ()))
NN = (((1,), (0,)), ((), ()))


def split_table(table):
    table = np.asarray(table, np.float32)
    high = table.astype(BF16)
    return high, (table - high.astype(np.float32)).astype(BF16)


def operators(height, width):
    slope, curve = gll_tables()
    tall = np.eye(height // 8)
    eye = np.eye(8)
    left = np.concatenate(
        [
            np.kron(tall, np.kron(eye, slope)),
            np.kron(tall, np.kron(slope, eye)),
            np.kron(tall, np.kron(eye, curve) + np.kron(curve, eye)),
        ]
    )
    high, low = split_table(left)
    left = np.concatenate([high, high, low], 1)
    cols = np.eye(width // 8)
    along, twice = np.kron(cols, slope), np.kron(cols, curve)
    high, low = split_table(np.concatenate([along.T, twice.T], 1))
    right = np.concatenate([high, high, low], 0)
    rows = face_rows(width)
    nodes = list(range(0, width, 8)) + [width - 1]
    face = np.zeros((-(-3 * rows // 16) * 16, width))
    for at, table in enumerate([np.eye(width), along, twice]):
        face[at * rows : at * rows + len(nodes)] = table[nodes]
    high, low = split_table(face)
    face = np.concatenate([high, high, low], 1)
    return np.concatenate([left, right], 1), face


def face_rows(width):
    return -(-(width // 8 + 1) // 8) * 8


def halves(value):
    high = value.astype(BF16)
    return high, (value - high.astype(F32)).astype(BF16)


def dot(left, right, dims=NN):
    return lax.dot_general(left, right, dims, preferred_element_type=F32)


def iota(shape, dim):
    return lax.broadcasted_iota(jnp.int32, shape, dim)


def split_index(value, size):
    if size & (size - 1) == 0:
        return value >> (size.bit_length() - 1), value & (size - 1)
    return value // size, value % size


def rate_of(vel, grad, lap):
    strain = grad[0][0] * grad[0][0] + grad[1][1] * grad[1][1] + grad[2][2] * grad[2][2]
    for one, two in ((0, 1), (0, 2), (1, 2)):
        both = grad[one][two] + grad[two][one]
        strain = strain + 0.5 * (both * both)
    eddy = viscosity + smagorinsky * jnp.sqrt(2.0 * strain + 1e-06)
    return [
        eddy * lap[c] - (vel[0] * grad[0][c] + vel[1] * grad[1][c] + vel[2] * grad[2][c])
        for c in range(3)
    ]


def step_kernel(
    across,
    along,
    sec_hbm,
    rotor_hbm,
    entry_hbm,
    count_ref,
    mortar_hbm,
    ops_hbm,
    face_hbm,
    start_hbm,
    pre_ref,
    lefts_ref,
    spread_ref,
    start_ref,
    sec_ref,
    rotor_ref,
    entry_ref,
    mortar_ref,
    ops_ref,
    face_ref,
    load_sem,
    sec_sem,
    table_ref,
    weight_ref,
    chosen_ref,
    split_ref,
    small_ref,
    side_ref,
    rate_ref,
    yz_ref,
    x_ref,
    merged_ref,
    edge_ref,
    edge_in_ref,
    row_ref,
    row_in_ref,
    panel_sem,
    edge_send,
    edge_recv,
    row_send,
    row_recv,
):
    _, depth, height, width = sec_ref.shape
    layers, tall = depth // 8, height // 8
    plane = 8 * height
    columns = layers * tall * width
    slots = rotor_ref.shape[1]
    packed = slots // 2
    shift = packed.bit_length() - 1
    entries = entry_ref.shape[2]
    pairs = entries // 2
    blocks = mortar_ref.shape[0]
    lanes_x = width // 8
    rows = face_rows(width)
    gx = lax.axis_index("gx")
    gy = lax.axis_index("gy")
    has_x = (gx > 0, gx < across - 1)
    has_y = (gy > 0, gy < along - 1)

    def number(flag):
        return jnp.where(flag, 1, 0)

    group = 2 if layers % 2 == 0 else 1
    groups = layers // group
    scale = 2.0 / 3.0 * time_step

    def sec_load(at):
        span = pl.ds(pl.multiple_of(at * group * 8, 8), group * 8)
        return pltpu.make_async_copy(sec_hbm.at[:, span], sec_ref.at[:, span], sec_sem.at[at])

    def load(at, source, target):
        return pltpu.make_async_copy(source, target, load_sem.at[at])

    face_load = load(0, face_hbm, face_ref)
    ops_load = load(1, ops_hbm, ops_ref)
    rotor_load = load(2, rotor_hbm, rotor_ref)
    entry_load = load(0, entry_hbm, entry_ref)
    mortar_load = load(1, mortar_hbm, mortar_ref)
    start_load = load(2, start_hbm, start_ref)
    face_load.start()
    for at in range(groups):
        sec_load(at).start()
    ops_load.start()
    rotor_load.start()

    barrier = pltpu.get_barrier_semaphore()
    for d in range(1, across):
        pl.semaphore_signal(
            barrier, inc=1, device_id={"gx": lax.rem(gx + d, across)}, device_id_type=MESH
        )
    for b in range(2):
        for dx in (-1, 0, 1):
            there = has_y[b] if dx == 0 else has_y[b] & has_x[(dx + 1) // 2]

            @pl.when(there)
            def _(b=b, dx=dx):
                pl.semaphore_signal(
                    barrier,
                    inc=1,
                    device_id={"gx": gx + dx, "gy": gy + 2 * b - 1},
                    device_id_type=MESH,
                )

    face_load.wait()
    for at in range(groups):
        sec_load(at).wait()
        for c in range(3):
            both = []
            for q in range(group):
                stack = sec_ref[c, pl.ds((at * group + q) * 8, 8)]
                value = jnp.concatenate(
                    [stack[:, 8 * j : 8 * j + 8].reshape(64, width) for j in range(tall)], 0
                )
                high, low = halves(value)
                split_ref[c, at * group + q, :, pl.ds(0, width)] = high
                split_ref[c, at * group + q, :, pl.ds(width, width)] = low
                both.append(jnp.concatenate([high, low, high], 1))
            small_ref[c, at] = dot(face_ref[...], jnp.concatenate(both, 0), NT)
    entry_load.start()
    ops_load.wait()
    mortar_load.start()
    left = pl.ds(0, 3 * plane)
    right = pl.ds(3 * plane, 2 * width)
    values = jnp.concatenate(
        [
            small_ref[c, k // group, pl.ds(0, rows), pl.ds(k % group * plane, plane)]
            for k in range(layers)
            for c in range(3)
        ],
        0,
    )
    high, low = halves(values)
    side_ref[...] = dot(jnp.concatenate([high, low, high], 1), ops_ref[:, left], NT)
    for k in range(layers):
        vel, grad, lap = [], [[], [], []], []
        for c in range(3):
            lanes = pl.ds(k % group * plane, plane)
            own_rows = pl.ds((k * 3 + c) * rows, rows)
            vel.append(small_ref[c, k // group, pl.ds(0, rows), lanes])
            grad[0].append(small_ref[c, k // group, pl.ds(rows, rows), lanes])
            grad[1].append(side_ref[own_rows, pl.ds(0, plane)])
            grad[2].append(side_ref[own_rows, pl.ds(plane, plane)])
            lap.append(
                small_ref[c, k // group, pl.ds(2 * rows, rows), lanes]
                + side_ref[own_rows, pl.ds(2 * plane, plane)]
            )
        for c, rate in enumerate(rate_of(vel, grad, lap)):
            rate_ref[pl.ds((c * layers + k) * rows, rows), :] = rate

    rotor_load.wait()
    start_load.start()
    square = iota((slots, slots), 0) == iota((slots, slots), 1)
    faces = jnp.broadcast_to(rotor_ref[...].astype(F32), (slots, slots))
    faces = jnp.sum(jnp.where(square, faces, 0.0), axis=1, keepdims=True).astype(jnp.int32)
    rest, face_x = split_index(faces, lanes_x)
    face_z, face_y = split_index(rest, tall)
    line = layers * rows
    pick = jnp.where(iota((slots, line), 1) == face_z * rows + face_x, 1.0, 0.0).astype(BF16)
    parts = []
    for c in range(3):
        high, low = halves(rate_ref[pl.ds(c * line, line), :])
        parts.append(jnp.concatenate([high, low], 0))
    found = dot(jnp.concatenate([pick, pick], 1), jnp.concatenate(parts, 1))
    own_half = iota((slots, plane), 1) >> 6 == face_y
    for c in range(3):
        value = jnp.where(own_half, found[:, c * plane : c * plane + plane], 0.0)
        value = value + pltpu.roll(value, 64, 1)
        table_ref[gx, c] = jnp.where(
            iota((packed, plane), 1) < 64, value[:packed], value[packed:]
        )
        for a in range(2):
            edge_ref[a, c] = jnp.zeros(edge_ref.shape[2:], F32)
            edge_ref[a, c, pl.ds(0, layers)] = rate_ref[
                pl.ds(c * line + a * lanes_x, layers, stride=rows), :
            ]

    expected = across - 1
    for b in range(2):
        expected = expected + number(has_y[b]) * (1 + number(has_x[0]) + number(has_x[1]))
    pl.semaphore_wait(barrier, expected)

    def edge_copy(a, dy):
        return pltpu.make_async_remote_copy(
            src_ref=edge_ref.at[a],
            dst_ref=edge_in_ref.at[1 - a, 1 - dy],
            send_sem=edge_send.at[a],
            recv_sem=edge_recv.at[1 - a],
            device_id={"gx": gx + 2 * a - 1, "gy": gy + dy},
            device_id_type=MESH,
        )

    def edge_there(a, dy):
        return has_x[a] if dy == 0 else has_x[a] & has_y[(dy + 1) // 2]

    for d in range(1, across):
        pltpu.make_async_remote_copy(
            src_ref=table_ref.at[gx],
            dst_ref=table_ref.at[gx],
            send_sem=panel_sem.at[0],
            recv_sem=panel_sem.at[1],
            device_id={"gx": lax.rem(gx + d, across)},
            device_id_type=MESH,
        ).start()

    edge_list = [(a, dy) for a in range(2) for dy in (-1, 0, 1)]
    for a, dy in edge_list:

        @pl.when(edge_there(a, dy))
        def _(a=a, dy=dy):
            edge_copy(a, dy).start()

        @pl.when(jnp.logical_not(edge_there(a, dy)))
        def _(a=a, dy=dy):
            edge_in_ref[a, dy + 1] = jnp.zeros(edge_in_ref.shape[2:], F32)

    lane = iota((8, width), 1)
    y_at = iota((8, width), 0)
    y8 = lane & 7
    own = jnp.where((y8 == 0) | (y8 == 7), 0.5, 1.0)
    own = jnp.where((lane == 0) & jnp.logical_not(has_x[0]), 1.0, own)
    own = jnp.where((lane == width - 1) & jnp.logical_not(has_x[1]), 1.0, own)
    other = jnp.where(((y8 == 0) & (lane > 0)) | ((y8 == 7) & (lane < width - 1)), 0.5, 0.0)

    def row_copy(b, at):
        return pltpu.make_async_remote_copy(
            src_ref=row_ref.at[b, at],
            dst_ref=row_in_ref.at[1 - b, at],
            send_sem=row_send.at[b],
            recv_sem=row_recv.at[1 - b],
            device_id={"gy": gy + 2 * b - 1},
            device_id_type=MESH,
        )

    def products(at):
        for c in range(3):
            pieces = [split_ref[c, at * group + q] for q in range(group)]
            wide = jnp.concatenate(pieces, 0)
            high, low = wide[:, :width], wide[:, width:]
            x_ref[at, c] = dot(jnp.concatenate([high, low, high], 1), ops_ref[:, right])
            high = jnp.concatenate([piece[:, :width] for piece in pieces], 1)
            low = jnp.concatenate([piece[:, width:] for piece in pieces], 1)
            yz_ref[at, c] = dot(ops_ref[:, left], jnp.concatenate([high, low, high], 0))

    def layer_group(at):
        for q in range(group):
            lanes = pl.ds(q * width, width)
            for z in range(8):
                z_at = (at * group + q) * 8 + z
                found = []
                for j in range(tall):
                    spot = j * 64 + 8 * z
                    x_rows = pl.ds(q * plane + spot, 8)
                    vel = [sec_ref[c, z_at, pl.ds(8 * j, 8)] for c in range(3)]
                    grad, lap = [[], [], []], []
                    for c in range(3):
                        grad[0].append(x_ref[at, c, x_rows, pl.ds(0, width)])
                        grad[1].append(yz_ref[at, c, pl.ds(spot, 8), lanes])
                        grad[2].append(yz_ref[at, c, pl.ds(plane + spot, 8), lanes])
                        lap.append(
                            x_ref[at, c, x_rows, pl.ds(width, width)]
                            + yz_ref[at, c, pl.ds(2 * plane + spot, 8), lanes]
                        )
                    merged = []
                    for rate in rate_of(vel, grad, lap):
                        partner = jnp.where(
                            y8 == 0, pltpu.roll(rate, 1, 1), pltpu.roll(rate, width - 1, 1)
                        )
                        merged.append(own * rate + other * partner)
                    found.append(merged)
                for c in range(3):
                    at_row = (c * depth + z_at) * height
                    row_ref[0, at, c, pl.ds(q * 8 + z, 1)] = found[0][c][0:1]
                    row_ref[1, at, c, pl.ds(q * 8 + z, 1)] = found[tall - 1][c][7:8]
                    for j in range(tall):
                        value = found[j][c]
                        if j > 0:
                            mean = 0.5 * (value + pltpu.roll(found[j - 1][c], 1, 0))
                            value = jnp.where(y_at == 0, mean, value)
                        if j < tall - 1:
                            mean = 0.5 * (value + pltpu.roll(found[j + 1][c], 7, 0))
                            value = jnp.where(y_at == 7, mean, value)
                        merged_ref[pl.ds(at_row + 8 * j, 8), :] = value
        for b in range(2):

            @pl.when(has_y[b])
            def _(b=b):
                row_copy(b, at).start()

    products(0)
    for at in range(groups):
        if at + 1 < groups:
            products(at + 1)
        layer_group(at)

    entry_load.wait()
    mortar_load.wait()
    start_load.wait()

    for c in range(3):
        for k in range(1, layers):
            top = pl.ds((c * depth + 8 * k - 1) * height, height)
            bottom = pl.ds((c * depth + 8 * k) * height, height)
            mean = 0.5 * (merged_ref[top, :] + merged_ref[bottom, :])
            merged_ref[top, :] = mean
            merged_ref[bottom, :] = mean

    entry_lane = iota((pairs, entries), 1)
    entry_row = 2 * iota((pairs, entries), 0)

    def upright(kind, odd_one):
        values = jnp.broadcast_to(entry_ref[kind].astype(F32), (pairs, entries))
        values = jnp.where(entry_lane == entry_row + odd_one, values, 0.0)
        return jnp.sum(values, axis=1, keepdims=True).astype(jnp.int32)

    live = 2 * iota((pairs, 1), 0) < count_ref[0, 0]
    stator = jnp.where(live, 8 * upright(0, 0), -1)
    spread = jnp.where(iota((pairs, columns), 1) == stator, 0.5, 0.0)
    factor = 1.0 - jnp.max(spread, axis=0, keepdims=True)
    spread_ref[pl.ds(0, pairs), :] = spread.astype(BF16)
    spread_ref[pl.ds(pairs, pairs), :] = spread.astype(BF16)
    row_e = iota((128, 1), 0)
    layer_e = row_e & 7
    side_e = (row_e >> 4) & 1
    tall_e = row_e >> 5
    kept = (tall_e < tall) & (layer_e < layers)
    kept = kept & (jnp.where(side_e == 0, number(has_x[0]), number(has_x[1])) > 0)
    to_e = jnp.where(kept, (layer_e * tall + tall_e) * width + side_e * (width - 1), -1)
    spread_ref[pl.ds(2 * pairs, 128), :] = jnp.where(
        iota((128, columns), 1) == to_e, 0.5 * factor, 0.0
    ).astype(BF16)

    for k in range(layers):
        for j in range(tall):
            at = (k * tall + j) * width
            keep = jnp.broadcast_to(scale * factor[:, at : at + width], (8, width))
            if j == 0:
                keep = jnp.where((y_at == 0) & has_y[0], 0.5 * keep, keep)
            if j == tall - 1:
                keep = jnp.where((y_at == 7) & has_y[1], 0.5 * keep, keep)
            for c in range(3):
                for z in range(8 * k, 8 * k + 8):
                    spot = pl.ds((c * depth + z) * height + 8 * j, 8)
                    pre_ref[spot, :] = (
                        start_ref[c, z, pl.ds(8 * j, 8)] * (1.0 / 3.0)
                        + sec_ref[c, z, pl.ds(8 * j, 8)] * (2.0 / 3.0)
                        + merged_ref[spot, :] * keep
                    )

    depth_k = blocks * 64
    for p in range(blocks // 2):
        high, low = halves(
            scale * jnp.concatenate([mortar_ref[2 * p], mortar_ref[2 * p + 1]], 1)
        )
        weight_ref[:, pl.ds(p * 128, 128)] = high
        weight_ref[:, pl.ds(depth_k + p * 128, 128)] = high
        weight_ref[:, pl.ds(2 * depth_k + p * 128, 128)] = low

    lane_half = iota((pairs, 128), 1) >> 6
    for odd_one in (0, 1):
        chosen = jnp.where(live, upright(2, odd_one), -1)
        for p in range(blocks // 2):
            chosen_ref[pl.ds(odd_one * pairs, pairs), pl.ds(p * 128, 128)] = jnp.where(
                chosen == lane_half + 2 * p, 1.0, 0.0
            ).astype(BF16)
    source = jnp.concatenate([upright(1, 0), upright(1, 1)], 0)
    spots = across * packed
    table_row = iota((2 * pairs, spots), 1)
    first_id = table_row + ((table_row >> shift) << shift)
    gather = jnp.where((source == first_id) | (source == first_id + packed), 1.0, 0.0).astype(BF16)
    source_half = (source >> shift) & 1
    straight = iota((2 * pairs, 128), 1) >> 6 == source_half
    take = jnp.where((iota((64, 128), 1) & 63) == iota((64, 128), 0), 1.0, 0.0).astype(BF16)

    e_lane = iota((8, 128), 1)
    e_row = iota((8, 128), 0)
    e_y = e_lane & 7
    e_z = (e_lane >> 3) & 7
    e_low = e_lane < 64
    many = 1 + number(has_y[0]) + number(has_y[1])
    for a in range(2):
        for n in range(1, 4):

            @pl.when(has_x[a] & (many == n))
            def _(a=a, n=n):
                came = edge_in_ref.at[a, pl.ds(0, n)]
                pltpu.make_async_remote_copy(
                    src_ref=came,
                    dst_ref=came,
                    send_sem=edge_send.at[a],
                    recv_sem=edge_recv.at[a],
                    device_id={"gx": gx + 2 * a - 1},
                    device_id_type=MESH,
                ).wait()

    y_move = ((e_y == 0) & (jnp.logical_not(e_low) | has_y[0])) | (
        (e_y == 7) & (e_low | has_y[1])
    )
    z_move = ((e_z == 0) & (e_row > 0)) | ((e_z == 7) & (e_row < layers - 1))
    for c in range(3):
        stack = []
        for a in range(2):
            mid = edge_in_ref[a, 1, c]
            near = jnp.where(
                e_y == 0,
                jnp.where(e_low, pltpu.roll(edge_in_ref[a, 0, c], 57, 1), pltpu.roll(mid, 57, 1)),
                jnp.where(e_low, pltpu.roll(mid, 71, 1), pltpu.roll(edge_in_ref[a, 2, c], 71, 1)),
            )
            mid = jnp.where(y_move, 0.5 * (mid + near), mid)
            near = jnp.where(
                e_z == 0,
                pltpu.roll(pltpu.roll(mid, 72, 1), 1, 0),
                pltpu.roll(pltpu.roll(mid, 56, 1), 7, 0),
            )
            mid = scale * jnp.where(z_move, 0.5 * (mid + near), mid)
            top = mid.astype(BF16).astype(F32)
            stack += [top, mid - top]
        stack = jnp.concatenate(stack, 0)
        low_stack = iota(stack.shape, 1) < 64
        stack = jnp.concatenate(
            [
                jnp.where(low_stack, stack, 0.0),
                jnp.where(low_stack, 0.0, stack),
                jnp.zeros((64, 128), F32),
            ],
            0,
        )
        lefts_ref[pl.ds(64 * c, 64), pl.ds(entries, 128)] = dot(
            take, stack.astype(BF16), NT
        ).astype(BF16)

    came = table_ref.at[pl.ds(0, across - 1)]
    pltpu.make_async_remote_copy(
        src_ref=came,
        dst_ref=came,
        send_sem=panel_sem.at[0],
        recv_sem=panel_sem.at[1],
        device_id={"gx": lax.rem(gx + 1, across)},
        device_id_type=MESH,
    ).wait()
    table = jnp.concatenate([table_ref[:, c].reshape(spots, 128) for c in range(3)], 1)
    high, low = halves(table)
    incoming = dot(jnp.concatenate([gather, gather], 1), jnp.concatenate([high, low], 0))
    for c in range(3):
        part = incoming[:, c * 128 : c * 128 + 128]
        high, low = halves(jnp.where(straight, part, pltpu.roll(part, 64, 1)))
        high = jnp.concatenate([high] * (blocks // 2), 1) * chosen_ref[...]
        low = jnp.concatenate([low] * (blocks // 2), 1) * chosen_ref[...]
        projected = dot(weight_ref[...], jnp.concatenate([high, low, high], 1), NT)
        projected = projected + pltpu.roll(projected, pairs, 1)
        top = projected.astype(BF16).astype(F32)
        first = iota(projected.shape, 1) < pairs
        lefts_ref[pl.ds(64 * c, 64), pl.ds(0, entries)] = jnp.where(
            first, top, projected - top
        ).astype(BF16)

    z_at = iota((depth, width), 0)
    z8 = z_at & 7
    z_low = (z8 == 0) & (z_at > 0)
    z_high = (z8 == 7) & (z_at < depth - 1)
    for b in range(2):

        @pl.when(has_y[b])
        def _(b=b):
            pltpu.make_async_remote_copy(
                src_ref=row_ref.at[b],
                dst_ref=row_in_ref.at[b],
                send_sem=row_send.at[b],
                recv_sem=row_recv.at[b],
                device_id={"gy": gy + 2 * b - 1},
                device_id_type=MESH,
            ).wait()
            j = b * (tall - 1)
            keep = jnp.concatenate(
                [
                    jnp.broadcast_to(
                        0.5 * scale * factor[:, (k * tall + j) * width : (k * tall + j + 1) * width],
                        (8, width),
                    )
                    for k in range(layers)
                ],
                0,
            )
            for c in range(3):
                value = jnp.concatenate([row_in_ref[b, at, c] for at in range(groups)], 0)
                near = jnp.where(
                    z_low, pltpu.roll(value, 1, 0), pltpu.roll(value, depth - 1, 0)
                )
                value = jnp.where(z_low | z_high, 0.5 * (value + near), value)
                spot = (pl.ds(c * depth * height + b * (height - 1), depth, stride=height), slice(None))
                pre_ref[spot] = pre_ref[spot] + keep * value


def finish_kernel(pre_ref, lefts_ref, spread_ref, out_hbm, out_ref, out_sem):
    _, depth, height, width = out_ref.shape
    layers, tall = depth // 8, height // 8
    for k in range(layers):
        change = dot(lefts_ref[...], spread_ref[:, pl.ds(k * tall * width, tall * width)])
        for c in range(3):
            for j in range(tall):
                for z in range(8):
                    row = 64 * c + 8 * z
                    out_ref[c, 8 * k + z, pl.ds(8 * j, 8)] = (
                        pre_ref[pl.ds((c * depth + 8 * k + z) * height + 8 * j, 8), :]
                        + change[row : row + 8, j * width : j * width + width]
                    )
        span = pl.ds(8 * k, 8)
        pltpu.make_async_copy(out_ref.at[:, span], out_hbm.at[:, span], out_sem).start()
    pltpu.make_async_copy(out_ref, out_hbm, out_sem).wait()


def local(initial, sectioned, rotor_faces, intersections, live_counts, mortar_blocks):
    across = lax.axis_size("gx")
    along = lax.axis_size("gy")
    _, depth, height, width = sectioned.shape
    ops, face = operators(height, width)
    plane = 8 * height
    layers = depth // 8
    columns = layers * (height // 8) * width
    group = 2 if layers % 2 == 0 else 1
    groups = layers // group
    packed = rotor_faces.shape[1] // 2
    entries = intersections.shape[1]
    blocks = mortar_blocks.shape[0]
    rows = face_rows(width)
    passed = [
        ((3 * depth * height, width), F32),
        ((3 * 64, entries + 128), BF16),
        ((entries + 128, columns), BF16),
    ]
    room = sum(int(np.prod(shape)) * jnp.dtype(kind).itemsize for shape, kind in passed)
    hbm, vmem = pl.BlockSpec(memory_space=pltpu.HBM), pl.BlockSpec(memory_space=pltpu.VMEM)
    staged = pl.pallas_call(
        functools.partial(step_kernel, across, along),
        out_shape=[pltpu.VMEM(shape, kind) for shape, kind in passed],
        in_specs=[hbm] * 3 + [pl.BlockSpec(memory_space=pltpu.SMEM)] + [hbm] * 4,
        out_specs=[vmem] * len(passed),
        scratch_shapes=[
            pltpu.VMEM(initial.shape, F32),
            pltpu.VMEM(sectioned.shape, F32),
            pltpu.VMEM(rotor_faces.shape, jnp.int32),
            pltpu.VMEM((3, 1, entries), jnp.int32),
            pltpu.VMEM(mortar_blocks.shape, F32),
            pltpu.VMEM(ops.shape, BF16),
            pltpu.VMEM(face.shape, BF16),
            pltpu.SemaphoreType.DMA((3,)),
            pltpu.SemaphoreType.DMA((groups,)),
            pltpu.VMEM((across, 3, packed, 128), F32),
            pltpu.VMEM((64, 3 * 64 * blocks), BF16),
            pltpu.VMEM((entries, 64 * blocks), BF16),
            pltpu.VMEM((3, layers, plane, 2 * width), BF16),
            pltpu.VMEM((3, groups, face.shape[0], group * plane), F32),
            pltpu.VMEM((3 * layers * rows, 3 * plane), F32),
            pltpu.VMEM((3 * layers * rows, plane), F32),
            pltpu.VMEM((groups, 3, 3 * plane, group * width), F32),
            pltpu.VMEM((groups, 3, group * plane, 2 * width), F32),
            pltpu.VMEM((3 * depth * height, width), F32),
            pltpu.VMEM((2, 3, 8, 128), F32),
            pltpu.VMEM((2, 3, 3, 8, 128), F32),
            pltpu.VMEM((2, groups, 3, group * 8, width), F32),
            pltpu.VMEM((2, groups, 3, group * 8, width), F32),
            pltpu.SemaphoreType.DMA((2,)),
            pltpu.SemaphoreType.DMA((2,)),
            pltpu.SemaphoreType.DMA((2,)),
            pltpu.SemaphoreType.DMA((2,)),
            pltpu.SemaphoreType.DMA((2,)),
        ],
        compiler_params=pltpu.CompilerParams(
            collective_id=0, has_side_effects=True, vmem_limit_bytes=67043328 - room
        ),
        name="step",
    )(
        sectioned,
        rotor_faces,
        jnp.transpose(intersections, (2, 0, 1)),
        live_counts,
        mortar_blocks,
        jnp.asarray(ops),
        jnp.asarray(face),
        initial,
    )
    return pl.pallas_call(
        finish_kernel,
        out_shape=jax.ShapeDtypeStruct(sectioned.shape, F32),
        in_specs=[vmem] * len(passed),
        out_specs=hbm,
        scratch_shapes=[pltpu.VMEM(sectioned.shape, F32), pltpu.SemaphoreType.DMA],
        compiler_params=pltpu.CompilerParams(vmem_limit_bytes=32 * 1024 * 1024),
        name="finish",
    )(*staged)


def solution(mesh):
    return jax.shard_map(
        local,
        mesh=mesh,
        in_specs=(
            P(None, None, "gy", "gx"),
            P(None, None, "gy", "gx"),
            P("gy", "gx"),
            P("gy", "gx", None),
            P("gy", "gx"),
            P(),
        ),
        out_specs=P(None, None, "gy", "gx"),
        check_vma=False,
    )
```

```python
import functools

import jax
import jax.numpy as jnp
import numpy as np
from jax import lax
from jax.experimental import pallas as pl
from jax.experimental.pallas import tpu as pltpu
from jax.sharding import PartitionSpec as P

time_step = 0.02
viscosity = 0.005
smagorinsky = 0.002
gll_interior = [
    -0.8717401485096066,
    -0.5917001814331423,
    -0.2092992179024789,
    0.2092992179024789,
    0.5917001814331423,
    0.8717401485096066,
]


def legendre_seven(points):
    lower_poly = points * 0.0 + 1.0
    current = points * 1.0
    for order_at in range(1, 7):
        following = ((2 * order_at + 1) * points * current - order_at * lower_poly) / (order_at + 1)
        lower_poly = current
        current = following
    return current


def gll_tables():
    degree = 7
    points = np.array([-1.0] + gll_interior + [1.0])
    values = legendre_seven(points)
    slope_table = np.zeros((degree + 1, degree + 1))
    for row_at in range(degree + 1):
        for col_at in range(degree + 1):
            if row_at != col_at:
                slope_table[row_at, col_at] = values[row_at] / (
                    values[col_at] * (points[row_at] - points[col_at])
                )
    slope_table[0, 0] = -degree * (degree + 1) / 4.0
    slope_table[degree, degree] = degree * (degree + 1) / 4.0
    return (slope_table, slope_table @ slope_table)


F32 = jnp.float32
BF16 = jnp.bfloat16
MESH = pl.DeviceIdType.MESH
NT = (((1,), (1,)), ((), ()))
NN = (((1,), (0,)), ((), ()))


def split_table(table):
    table = np.asarray(table, np.float32)
    high = table.astype(BF16)
    return high, (table - high.astype(np.float32)).astype(BF16)


def operators(height, width):
    slope, curve = gll_tables()
    tall = np.eye(height // 8)
    eye = np.eye(8)
    left = np.concatenate(
        [
            np.kron(tall, np.kron(eye, slope)),
            np.kron(tall, np.kron(slope, eye)),
            np.kron(tall, np.kron(eye, curve) + np.kron(curve, eye)),
        ]
    )
    left = np.concatenate(split_table(left), 1)
    cols = np.eye(width // 8)
    along, twice = np.kron(cols, slope), np.kron(cols, curve)
    right = np.concatenate(split_table(np.concatenate([along.T, twice.T], 1)), 0)
    rows = face_rows(width)
    nodes = list(range(0, width, 8)) + [width - 1]
    face = np.zeros((-(-3 * rows // 16) * 16, width))
    for at, table in enumerate([np.eye(width), along, twice]):
        face[at * rows : at * rows + len(nodes)] = table[nodes]
    return np.concatenate([left, right], 0), np.concatenate(split_table(face), 1)


def face_rows(width):
    return -(-(width // 8 + 1) // 8) * 8


def halves(value):
    high = value.astype(BF16)
    return high, (value - high.astype(F32)).astype(BF16)


def dot(left, right, dims=NN):
    return lax.dot_general(left, right, dims, preferred_element_type=F32)


def iota(shape, dim):
    return lax.broadcasted_iota(jnp.int32, shape, dim)


def split_index(value, size):
    if size & (size - 1) == 0:
        return value >> (size.bit_length() - 1), value & (size - 1)
    return value // size, value % size


def rate_of(vel, grad, lap):
    strain = grad[0][0] * grad[0][0] + grad[1][1] * grad[1][1] + grad[2][2] * grad[2][2]
    strain = 2.0 * strain + 1e-06
    for one, two in ((0, 1), (0, 2), (1, 2)):
        both = grad[one][two] + grad[two][one]
        strain = strain + both * both
    eddy = viscosity + smagorinsky * (strain * lax.rsqrt(strain))
    return [
        eddy * lap[c] - (vel[0] * grad[0][c] + vel[1] * grad[1][c] + vel[2] * grad[2][c])
        for c in range(3)
    ]


def step_kernel(
    across,
    along,
    sec_hbm,
    rotor_hbm,
    entry_hbm,
    count_ref,
    mortar_hbm,
    ops_hbm,
    face_hbm,
    start_hbm,
    pre_ref,
    lefts_ref,
    spread_ref,
    start_ref,
    sec_ref,
    rotor_ref,
    entry_ref,
    mortar_ref,
    ops_ref,
    face_ref,
    load_sem,
    sec_sem,
    table_ref,
    weight_ref,
    chosen_ref,
    split_ref,
    small_ref,
    side_ref,
    thin_ref,
    yz_ref,
    x_ref,
    merged_ref,
    edge_ref,
    edge_in_ref,
    row_ref,
    row_in_ref,
    panel_sem,
    edge_send,
    edge_recv,
    row_send,
    row_recv,
):
    _, depth, height, width = sec_ref.shape
    layers, tall = depth // 8, height // 8
    plane = 8 * height
    columns = layers * tall * width
    slots = rotor_ref.shape[1]
    packed = slots // 2
    shift = packed.bit_length() - 1
    entries = entry_ref.shape[2]
    pairs = entries // 2
    blocks = mortar_ref.shape[0]
    lanes_x = width // 8
    rows = face_rows(width)
    gx = lax.axis_index("gx")
    gy = lax.axis_index("gy")
    has_x = (gx > 0, gx < across - 1)
    has_y = (gy > 0, gy < along - 1)

    def number(flag):
        return jnp.where(flag, 1, 0)

    group = 2 if layers % 2 == 0 else 1
    groups = layers // group
    scale = 2.0 / 3.0 * time_step

    def sec_load(at):
        span = pl.ds(pl.multiple_of(at * group * 8, 8), group * 8)
        return pltpu.make_async_copy(sec_hbm.at[:, span], sec_ref.at[:, span], sec_sem.at[at])

    def load(at, source, target):
        return pltpu.make_async_copy(source, target, load_sem.at[at])

    face_load = load(0, face_hbm, face_ref)
    ops_load = load(1, ops_hbm, ops_ref)
    rotor_load = load(2, rotor_hbm, rotor_ref)
    entry_load = load(0, entry_hbm, entry_ref)
    mortar_load = load(1, mortar_hbm, mortar_ref)
    start_load = load(2, start_hbm, start_ref)
    face_load.start()
    for at in range(groups):
        sec_load(at).start()
    ops_load.start()
    rotor_load.start()

    barrier = pltpu.get_barrier_semaphore()
    for d in range(1, across):
        pl.semaphore_signal(
            barrier, inc=1, device_id={"gx": lax.rem(gx + d, across)}, device_id_type=MESH
        )
    for b in range(2):
        for dx in (-1, 0, 1):
            there = has_y[b] if dx == 0 else has_y[b] & has_x[(dx + 1) // 2]

            @pl.when(there)
            def _(b=b, dx=dx):
                pl.semaphore_signal(
                    barrier,
                    inc=1,
                    device_id={"gx": gx + dx, "gy": gy + 2 * b - 1},
                    device_id_type=MESH,
                )

    def tripled(left_ref, span, size):
        high = left_ref[span, pl.ds(0, size)]
        return jnp.concatenate([high, high, left_ref[span, pl.ds(size, size)]], 1)

    line = layers * lanes_x
    face_load.wait()
    for at in range(groups):
        if at == 0:
            sec_load(at).wait()
        if at == min(1, groups - 1):
            for later in range(1, groups):
                sec_load(later).wait()
            ops_load.wait()
            rotor_load.wait()
            entry_load.start()
            mortar_load.start()
            start_load.start()
        for c in range(3):
            both = []
            for q in range(group):
                stack = sec_ref[c, pl.ds((at * group + q) * 8, 8)]
                value = jnp.concatenate(
                    [stack[:, 8 * j : 8 * j + 8].reshape(64, width) for j in range(tall)], 0
                )
                high, low = halves(value)
                split_ref[c, at * group + q, :, pl.ds(0, width)] = high
                split_ref[c, at * group + q, :, pl.ds(width, width)] = low
                both.append(jnp.concatenate([high, low, high], 1))
            small_ref[c, at] = dot(
                tripled(face_ref, slice(None), width), jnp.concatenate(both, 0), NT
            )
    square = iota((slots, slots), 0) == iota((slots, slots), 1)
    faces = jnp.broadcast_to(rotor_ref[...].astype(F32), (slots, slots))
    faces = jnp.sum(jnp.where(square, faces, 0.0), axis=1, keepdims=True).astype(jnp.int32)
    rest, face_x = split_index(faces, lanes_x)
    face_z, face_y = split_index(rest, tall)
    target = face_z * lanes_x + face_x
    pick = iota((slots, 2 * line), 1)
    pick = jnp.where((pick == target) | (pick == target + line), 1.0, 0.0).astype(BF16)

    def small_rows(c, k, first, count):
        return small_ref[c, k // group, pl.ds(first, count), pl.ds(k % group * plane, plane)]

    parts = []
    for kind in range(3):
        for c in range(3):
            high, low = halves(
                jnp.concatenate(
                    [small_rows(c, k, kind * rows, lanes_x) for k in range(layers)], 0
                )
            )
            parts.append(jnp.concatenate([high, low], 0))
            thin_ref[kind, c, pl.ds(slots, 16)] = jnp.zeros((16, plane), F32)
            for a in range(2):
                for k in range(layers):
                    thin_ref[kind, c, pl.ds(slots + 8 * a + k, 1)] = small_rows(
                        c, k, kind * rows + a * lanes_x, 1
                    )
    found = dot(pick, jnp.concatenate(parts, 1))
    for kind in range(3):
        for c in range(3):
            at = (kind * 3 + c) * plane
            thin_ref[kind, c, pl.ds(0, slots)] = found[:, at : at + plane]
    left = tripled(ops_ref, pl.ds(0, 3 * plane), plane)
    high, low = halves(jnp.concatenate([thin_ref[0, c] for c in range(3)], 0))
    side_ref[...] = dot(jnp.concatenate([high, low, high], 1), left, NT)
    thin = slots + 16
    own_half = iota((slots, plane), 1) >> 6 == face_y
    grad = [
        [thin_ref[1, c] for c in range(3)],
        [side_ref[pl.ds(c * thin, thin), pl.ds(0, plane)] for c in range(3)],
        [side_ref[pl.ds(c * thin, thin), pl.ds(plane, plane)] for c in range(3)],
    ]
    lap = [
        thin_ref[2, c] + side_ref[pl.ds(c * thin, thin), pl.ds(2 * plane, plane)]
        for c in range(3)
    ]
    for c, rate in enumerate(rate_of([thin_ref[0, c] for c in range(3)], grad, lap)):
        value = jnp.where(own_half, rate[:slots], 0.0)
        value = value + pltpu.roll(value, 64, 1)
        table_ref[gx, c] = jnp.where(
            iota((packed, plane), 1) < 64, value[:packed], value[packed:]
        )
        edge_ref[0, c] = rate[slots : slots + 8]
        edge_ref[1, c] = rate[slots + 8 :]

    expected = across - 1
    for b in range(2):
        expected = expected + number(has_y[b]) * (1 + number(has_x[0]) + number(has_x[1]))
    pl.semaphore_wait(barrier, expected)

    def edge_copy(a, dy):
        return pltpu.make_async_remote_copy(
            src_ref=edge_ref.at[a],
            dst_ref=edge_in_ref.at[1 - a, 1 - dy],
            send_sem=edge_send.at[a],
            recv_sem=edge_recv.at[1 - a],
            device_id={"gx": gx + 2 * a - 1, "gy": gy + dy},
            device_id_type=MESH,
        )

    def edge_there(a, dy):
        return has_x[a] if dy == 0 else has_x[a] & has_y[(dy + 1) // 2]

    edge_list = [(a, dy) for a in range(2) for dy in (-1, 0, 1)]
    for a, dy in edge_list:

        @pl.when(edge_there(a, dy))
        def _(a=a, dy=dy):
            edge_copy(a, dy).start()

        @pl.when(jnp.logical_not(edge_there(a, dy)))
        def _(a=a, dy=dy):
            edge_in_ref[a, dy + 1] = jnp.zeros(edge_in_ref.shape[2:], F32)

    for d in range(1, across):
        pltpu.make_async_remote_copy(
            src_ref=table_ref.at[gx],
            dst_ref=table_ref.at[gx],
            send_sem=panel_sem.at[0],
            recv_sem=panel_sem.at[1],
            device_id={"gx": lax.rem(gx + d, across)},
            device_id_type=MESH,
        ).start()

    lane = iota((8, width), 1)
    y_at = iota((8, width), 0)
    y8 = lane & 7
    own = jnp.where((y8 == 0) | (y8 == 7), 0.5, 1.0)
    own = jnp.where((lane == 0) & jnp.logical_not(has_x[0]), 1.0, own)
    own = jnp.where((lane == width - 1) & jnp.logical_not(has_x[1]), 1.0, own)
    other = jnp.where(((y8 == 0) & (lane > 0)) | ((y8 == 7) & (lane < width - 1)), 0.5, 0.0)

    def row_copy(b, at):
        return pltpu.make_async_remote_copy(
            src_ref=row_ref.at[b, at],
            dst_ref=row_in_ref.at[1 - b, at],
            send_sem=row_send.at[b],
            recv_sem=row_recv.at[1 - b],
            device_id={"gy": gy + 2 * b - 1},
            device_id_type=MESH,
        )

    def products(at):
        high = ops_ref[pl.ds(3 * plane, width)]
        right = jnp.concatenate([high, high, ops_ref[pl.ds(3 * plane + width, width)]], 0)
        left = tripled(ops_ref, pl.ds(0, 3 * plane), plane)
        for c in range(3):
            pieces = [split_ref[c, at * group + q] for q in range(group)]
            wide = jnp.concatenate(pieces, 0)
            high, low = wide[:, :width], wide[:, width:]
            x_ref[at, c] = dot(jnp.concatenate([high, low, high], 1), right)
            high = jnp.concatenate([piece[:, :width] for piece in pieces], 1)
            low = jnp.concatenate([piece[:, width:] for piece in pieces], 1)
            yz_ref[at, c] = dot(left, jnp.concatenate([high, low, high], 0))

    def layer_group(at):
        for q in range(group):
            lanes = pl.ds(q * width, width)
            for z in range(8):
                z_at = (at * group + q) * 8 + z
                found = []
                for j in range(tall):
                    spot = j * 64 + 8 * z
                    x_rows = pl.ds(q * plane + spot, 8)
                    vel = [sec_ref[c, z_at, pl.ds(8 * j, 8)] for c in range(3)]
                    grad, lap = [[], [], []], []
                    for c in range(3):
                        grad[0].append(x_ref[at, c, x_rows, pl.ds(0, width)])
                        grad[1].append(yz_ref[at, c, pl.ds(spot, 8), lanes])
                        grad[2].append(yz_ref[at, c, pl.ds(plane + spot, 8), lanes])
                        lap.append(
                            x_ref[at, c, x_rows, pl.ds(width, width)]
                            + yz_ref[at, c, pl.ds(2 * plane + spot, 8), lanes]
                        )
                    merged = []
                    for rate in rate_of(vel, grad, lap):
                        partner = jnp.where(
                            y8 == 0, pltpu.roll(rate, 1, 1), pltpu.roll(rate, width - 1, 1)
                        )
                        merged.append(own * rate + other * partner)
                    found.append(merged)
                for c in range(3):
                    at_row = (c * depth + z_at) * height
                    row_ref[0, at, c, pl.ds(q * 8 + z, 1)] = found[0][c][0:1]
                    row_ref[1, at, c, pl.ds(q * 8 + z, 1)] = found[tall - 1][c][7:8]
                    for j in range(tall):
                        value = found[j][c]
                        if j > 0:
                            mean = 0.5 * (value + pltpu.roll(found[j - 1][c], 1, 0))
                            value = jnp.where(y_at == 0, mean, value)
                        if j < tall - 1:
                            mean = 0.5 * (value + pltpu.roll(found[j + 1][c], 7, 0))
                            value = jnp.where(y_at == 7, mean, value)
                        merged_ref[pl.ds(at_row + 8 * j, 8), :] = value
        for b in range(2):

            @pl.when(has_y[b])
            def _(b=b):
                row_copy(b, at).start()

    products(0)
    for at in range(groups):
        if at + 1 < groups:
            products(at + 1)
        layer_group(at)

    entry_load.wait()
    mortar_load.wait()
    start_load.wait()

    for c in range(3):
        for k in range(1, layers):
            top = pl.ds((c * depth + 8 * k - 1) * height, height)
            bottom = pl.ds((c * depth + 8 * k) * height, height)
            mean = 0.5 * (merged_ref[top, :] + merged_ref[bottom, :])
            merged_ref[top, :] = mean
            merged_ref[bottom, :] = mean

    entry_lane = iota((pairs, entries), 1)
    entry_row = 2 * iota((pairs, entries), 0)

    def upright(kind, odd_one):
        values = jnp.broadcast_to(entry_ref[kind].astype(F32), (pairs, entries))
        values = jnp.where(entry_lane == entry_row + odd_one, values, 0.0)
        return jnp.sum(values, axis=1, keepdims=True).astype(jnp.int32)

    live = 2 * iota((pairs, 1), 0) < count_ref[0, 0]
    stator = jnp.where(live, 8 * upright(0, 0), -1)
    spread = jnp.where(iota((pairs, columns), 1) == stator, 0.5, 0.0)
    factor = 1.0 - jnp.max(spread, axis=0, keepdims=True)
    spread_ref[pl.ds(0, pairs), :] = spread.astype(BF16)
    spread_ref[pl.ds(pairs, pairs), :] = spread.astype(BF16)
    row_e = iota((128, 1), 0)
    layer_e = row_e & 7
    side_e = (row_e >> 4) & 1
    tall_e = row_e >> 5
    kept = (tall_e < tall) & (layer_e < layers)
    kept = kept & (jnp.where(side_e == 0, number(has_x[0]), number(has_x[1])) > 0)
    to_e = jnp.where(kept, (layer_e * tall + tall_e) * width + side_e * (width - 1), -1)
    spread_ref[pl.ds(2 * pairs, 128), :] = jnp.where(
        iota((128, columns), 1) == to_e, 0.5 * factor, 0.0
    ).astype(BF16)

    for k in range(layers):
        for j in range(tall):
            at = (k * tall + j) * width
            keep = jnp.broadcast_to(scale * factor[:, at : at + width], (8, width))
            if j == 0:
                keep = jnp.where((y_at == 0) & has_y[0], 0.5 * keep, keep)
            if j == tall - 1:
                keep = jnp.where((y_at == 7) & has_y[1], 0.5 * keep, keep)
            for c in range(3):
                for z in range(8 * k, 8 * k + 8):
                    spot = pl.ds((c * depth + z) * height + 8 * j, 8)
                    pre_ref[spot, :] = (
                        start_ref[c, z, pl.ds(8 * j, 8)] * (1.0 / 3.0)
                        + sec_ref[c, z, pl.ds(8 * j, 8)] * (2.0 / 3.0)
                        + merged_ref[spot, :] * keep
                    )

    for b in range(blocks):
        high, low = halves(scale * mortar_ref[b])
        weight_ref[pl.ds(64 * b, 64)] = jnp.concatenate(
            [high, high, low, jnp.zeros((64, 64), BF16)], 1
        )

    lane_half = iota((pairs, 128), 1) >> 6
    for odd_one in (0, 1):
        chosen = jnp.where(live, upright(2, odd_one), -1)
        for p in range(blocks // 2):
            chosen_ref[pl.ds(odd_one * pairs, pairs), pl.ds(p * 128, 128)] = jnp.where(
                chosen == lane_half + 2 * p, 1.0, 0.0
            )
    source = jnp.concatenate([upright(1, 0), upright(1, 1)], 0)
    spots = across * packed
    table_row = iota((2 * pairs, spots), 1)
    first_id = table_row + ((table_row >> shift) << shift)
    gather = jnp.where((source == first_id) | (source == first_id + packed), 1.0, 0.0).astype(BF16)
    source_half = (source >> shift) & 1
    straight = iota((2 * pairs, 128), 1) >> 6 == source_half
    take = jnp.where((iota((64, 128), 1) & 63) == iota((64, 128), 0), 1.0, 0.0).astype(BF16)

    e_lane = iota((8, 128), 1)
    e_row = iota((8, 128), 0)
    e_y = e_lane & 7
    e_z = (e_lane >> 3) & 7
    e_low = e_lane < 64
    many = 1 + number(has_y[0]) + number(has_y[1])
    for a in range(2):
        for n in range(1, 4):

            @pl.when(has_x[a] & (many == n))
            def _(a=a, n=n):
                came = edge_in_ref.at[a, pl.ds(0, n)]
                pltpu.make_async_remote_copy(
                    src_ref=came,
                    dst_ref=came,
                    send_sem=edge_send.at[a],
                    recv_sem=edge_recv.at[a],
                    device_id={"gx": gx + 2 * a - 1},
                    device_id_type=MESH,
                ).wait()

    y_move = ((e_y == 0) & (jnp.logical_not(e_low) | has_y[0])) | (
        (e_y == 7) & (e_low | has_y[1])
    )
    z_move = ((e_z == 0) & (e_row > 0)) | ((e_z == 7) & (e_row < layers - 1))
    for c in range(3):
        stack = []
        for a in range(2):
            mid = edge_in_ref[a, 1, c]
            near = jnp.where(
                e_y == 0,
                jnp.where(e_low, pltpu.roll(edge_in_ref[a, 0, c], 57, 1), pltpu.roll(mid, 57, 1)),
                jnp.where(e_low, pltpu.roll(mid, 71, 1), pltpu.roll(edge_in_ref[a, 2, c], 71, 1)),
            )
            mid = jnp.where(y_move, 0.5 * (mid + near), mid)
            near = jnp.where(
                e_z == 0,
                pltpu.roll(pltpu.roll(mid, 72, 1), 1, 0),
                pltpu.roll(pltpu.roll(mid, 56, 1), 7, 0),
            )
            mid = scale * jnp.where(z_move, 0.5 * (mid + near), mid)
            top = mid.astype(BF16).astype(F32)
            stack += [top, mid - top]
        stack = jnp.concatenate(stack, 0)
        low_stack = iota(stack.shape, 1) < 64
        stack = jnp.concatenate(
            [
                jnp.where(low_stack, stack, 0.0),
                jnp.where(low_stack, 0.0, stack),
                jnp.zeros((64, 128), F32),
            ],
            0,
        )
        lefts_ref[pl.ds(64 * c, 64), pl.ds(entries, 128)] = dot(
            take, stack.astype(BF16), NT
        ).astype(BF16)

    came = table_ref.at[pl.ds(0, across - 1)]
    pltpu.make_async_remote_copy(
        src_ref=came,
        dst_ref=came,
        send_sem=panel_sem.at[0],
        recv_sem=panel_sem.at[1],
        device_id={"gx": lax.rem(gx + 1, across)},
        device_id_type=MESH,
    ).wait()
    table = jnp.concatenate([table_ref[:, c].reshape(spots, 128) for c in range(3)], 1)
    high, low = halves(table)
    incoming = dot(jnp.concatenate([gather, gather], 1), jnp.concatenate([high, low], 0))
    low_lane = iota((entries, 128), 1) < 64
    spaced = []
    for c in range(3):
        part = incoming[:, c * 128 : c * 128 + 128]
        part = jnp.where(straight, part, pltpu.roll(part, 64, 1))
        top = part.astype(BF16).astype(F32)
        spaced.append(jnp.concatenate([jnp.where(low_lane, top, part - top), top], 1).astype(BF16))
    spaced = jnp.concatenate(spaced, 0)
    total = [0.0] * 3
    for p in range(blocks // 4):
        product = dot(spaced, weight_ref[pl.ds(256 * p, 256)], NT)
        for half in range(2):
            mask = chosen_ref[:, pl.ds(256 * p + 128 * half, 128)]
            for c in range(3):
                total[c] = total[c] + mask * product[
                    c * entries : (c + 1) * entries, 128 * half : 128 * half + 128
                ]
    stack = []
    for c in range(3):
        value = total[c][:pairs] + total[c][pairs:]
        value = value + pltpu.roll(value, 64, 1)
        top = value.astype(BF16).astype(F32)
        stack += [top, value - top]
    stack = jnp.concatenate(stack, 0).astype(BF16)
    take = jnp.where(iota((64, 128), 1) == iota((64, 128), 0), 1.0, 0.0).astype(BF16)
    turned = dot(take, stack, NT).astype(BF16)
    for c in range(3):
        lefts_ref[pl.ds(64 * c, 64), pl.ds(0, entries)] = turned[:, c * entries : (c + 1) * entries]

    z_at = iota((depth, width), 0)
    z8 = z_at & 7
    z_low = (z8 == 0) & (z_at > 0)
    z_high = (z8 == 7) & (z_at < depth - 1)
    for b in range(2):

        @pl.when(has_y[b])
        def _(b=b):
            pltpu.make_async_remote_copy(
                src_ref=row_ref.at[b],
                dst_ref=row_in_ref.at[b],
                send_sem=row_send.at[b],
                recv_sem=row_recv.at[b],
                device_id={"gy": gy + 2 * b - 1},
                device_id_type=MESH,
            ).wait()
            j = b * (tall - 1)
            keep = jnp.concatenate(
                [
                    jnp.broadcast_to(
                        0.5 * scale * factor[:, (k * tall + j) * width : (k * tall + j + 1) * width],
                        (8, width),
                    )
                    for k in range(layers)
                ],
                0,
            )
            for c in range(3):
                value = jnp.concatenate([row_in_ref[b, at, c] for at in range(groups)], 0)
                near = jnp.where(
                    z_low, pltpu.roll(value, 1, 0), pltpu.roll(value, depth - 1, 0)
                )
                value = jnp.where(z_low | z_high, 0.5 * (value + near), value)
                spot = (pl.ds(c * depth * height + b * (height - 1), depth, stride=height), slice(None))
                pre_ref[spot] = pre_ref[spot] + keep * value


def finish_kernel(pre_ref, lefts_ref, spread_ref, out_hbm, out_ref, out_sem):
    _, depth, height, width = out_ref.shape
    layers, tall = depth // 8, height // 8
    for k in range(layers):
        change = dot(lefts_ref[...], spread_ref[:, pl.ds(k * tall * width, tall * width)])
        for c in range(3):
            for j in range(tall):
                for z in range(8):
                    row = 64 * c + 8 * z
                    out_ref[c, 8 * k + z, pl.ds(8 * j, 8)] = (
                        pre_ref[pl.ds((c * depth + 8 * k + z) * height + 8 * j, 8), :]
                        + change[row : row + 8, j * width : j * width + width]
                    )
        span = pl.ds(8 * k, 8)
        pltpu.make_async_copy(out_ref.at[:, span], out_hbm.at[:, span], out_sem).start()
    pltpu.make_async_copy(out_ref, out_hbm, out_sem).wait()


def local(initial, sectioned, rotor_faces, intersections, live_counts, mortar_blocks):
    across = lax.axis_size("gx")
    along = lax.axis_size("gy")
    _, depth, height, width = sectioned.shape
    ops, face = operators(height, width)
    plane = 8 * height
    layers = depth // 8
    columns = layers * (height // 8) * width
    group = 2 if layers % 2 == 0 else 1
    groups = layers // group
    packed = rotor_faces.shape[1] // 2
    entries = intersections.shape[1]
    blocks = mortar_blocks.shape[0]
    passed = [
        ((3 * depth * height, width), F32),
        ((3 * 64, entries + 128), BF16),
        ((entries + 128, columns), BF16),
    ]
    room = sum(int(np.prod(shape)) * jnp.dtype(kind).itemsize for shape, kind in passed)
    hbm, vmem = pl.BlockSpec(memory_space=pltpu.HBM), pl.BlockSpec(memory_space=pltpu.VMEM)
    staged = pl.pallas_call(
        functools.partial(step_kernel, across, along),
        out_shape=[pltpu.VMEM(shape, kind) for shape, kind in passed],
        in_specs=[hbm] * 3 + [pl.BlockSpec(memory_space=pltpu.SMEM)] + [hbm] * 4,
        out_specs=[vmem] * len(passed),
        scratch_shapes=[
            pltpu.VMEM(initial.shape, F32),
            pltpu.VMEM(sectioned.shape, F32),
            pltpu.VMEM(rotor_faces.shape, jnp.int32),
            pltpu.VMEM((3, 1, entries), jnp.int32),
            pltpu.VMEM(mortar_blocks.shape, F32),
            pltpu.VMEM(ops.shape, BF16),
            pltpu.VMEM(face.shape, BF16),
            pltpu.SemaphoreType.DMA((3,)),
            pltpu.SemaphoreType.DMA((groups,)),
            pltpu.VMEM((across, 3, packed, 128), F32),
            pltpu.VMEM((64 * blocks, 256), BF16),
            pltpu.VMEM((entries, 64 * blocks), F32),
            pltpu.VMEM((3, layers, plane, 2 * width), BF16),
            pltpu.VMEM((3, groups, face.shape[0], group * plane), F32),
            pltpu.VMEM((3 * (rotor_faces.shape[1] + 16), 3 * plane), F32),
            pltpu.VMEM((3, 3, rotor_faces.shape[1] + 16, plane), F32),
            pltpu.VMEM((groups, 3, 3 * plane, group * width), F32),
            pltpu.VMEM((groups, 3, group * plane, 2 * width), F32),
            pltpu.VMEM((3 * depth * height, width), F32),
            pltpu.VMEM((2, 3, 8, 128), F32),
            pltpu.VMEM((2, 3, 3, 8, 128), F32),
            pltpu.VMEM((2, groups, 3, group * 8, width), F32),
            pltpu.VMEM((2, groups, 3, group * 8, width), F32),
            pltpu.SemaphoreType.DMA((2,)),
            pltpu.SemaphoreType.DMA((2,)),
            pltpu.SemaphoreType.DMA((2,)),
            pltpu.SemaphoreType.DMA((2,)),
            pltpu.SemaphoreType.DMA((2,)),
        ],
        compiler_params=pltpu.CompilerParams(
            collective_id=0, has_side_effects=True, vmem_limit_bytes=67043328 - room
        ),
        name="step",
    )(
        sectioned,
        rotor_faces,
        jnp.transpose(intersections, (2, 0, 1)),
        live_counts,
        mortar_blocks,
        jnp.asarray(ops),
        jnp.asarray(face),
        initial,
    )
    return pl.pallas_call(
        finish_kernel,
        out_shape=jax.ShapeDtypeStruct(sectioned.shape, F32),
        in_specs=[vmem] * len(passed),
        out_specs=hbm,
        scratch_shapes=[pltpu.VMEM(sectioned.shape, F32), pltpu.SemaphoreType.DMA],
        compiler_params=pltpu.CompilerParams(vmem_limit_bytes=32 * 1024 * 1024),
        name="finish",
    )(*staged)


def solution(mesh):
    return jax.shard_map(
        local,
        mesh=mesh,
        in_specs=(
            P(None, None, "gy", "gx"),
            P(None, None, "gy", "gx"),
            P("gy", "gx"),
            P("gy", "gx", None),
            P("gy", "gx"),
            P(),
        ),
        out_specs=P(None, None, "gy", "gx"),
        check_vma=False,
    )
```

```python
import functools

import jax
import jax.numpy as jnp
import numpy as np
from jax import lax
from jax.experimental import pallas as pl
from jax.experimental.pallas import tpu as pltpu
from jax.sharding import PartitionSpec as P

time_step = 0.02
viscosity = 0.005
smagorinsky = 0.002
gll_interior = [
    -0.8717401485096066,
    -0.5917001814331423,
    -0.2092992179024789,
    0.2092992179024789,
    0.5917001814331423,
    0.8717401485096066,
]


def legendre_seven(points):
    lower_poly = points * 0.0 + 1.0
    current = points * 1.0
    for order_at in range(1, 7):
        following = ((2 * order_at + 1) * points * current - order_at * lower_poly) / (order_at + 1)
        lower_poly = current
        current = following
    return current


def gll_tables():
    degree = 7
    points = np.array([-1.0] + gll_interior + [1.0])
    values = legendre_seven(points)
    slope_table = np.zeros((degree + 1, degree + 1))
    for row_at in range(degree + 1):
        for col_at in range(degree + 1):
            if row_at != col_at:
                slope_table[row_at, col_at] = values[row_at] / (
                    values[col_at] * (points[row_at] - points[col_at])
                )
    slope_table[0, 0] = -degree * (degree + 1) / 4.0
    slope_table[degree, degree] = degree * (degree + 1) / 4.0
    return (slope_table, slope_table @ slope_table)


F32 = jnp.float32
BF16 = jnp.bfloat16
MESH = pl.DeviceIdType.MESH
NT = (((1,), (1,)), ((), ()))
NN = (((1,), (0,)), ((), ()))


def split_table(table):
    table = np.asarray(table, np.float32)
    high = table.astype(BF16)
    return high, (table - high.astype(np.float32)).astype(BF16)


def operators(height, width):
    slope, curve = gll_tables()
    tall = np.eye(height // 8)
    eye = np.eye(8)
    left = np.concatenate(
        [
            np.kron(tall, np.kron(eye, slope)),
            np.kron(tall, np.kron(slope, eye)),
            np.kron(tall, np.kron(eye, curve) + np.kron(curve, eye)),
        ]
    )
    left = np.concatenate(split_table(left), 1)
    cols = np.eye(width // 8)
    along, twice = np.kron(cols, slope), np.kron(cols, curve)
    right = np.concatenate(split_table(np.concatenate([along.T, twice.T], 1)), 0)
    rows = face_rows(width)
    nodes = list(range(0, width, 8)) + [width - 1]
    face = np.zeros((-(-3 * rows // 16) * 16, width))
    for at, table in enumerate([np.eye(width), along, twice]):
        face[at * rows : at * rows + len(nodes)] = table[nodes]
    return np.concatenate([left, right], 0), np.concatenate(split_table(face), 1)


def face_rows(width):
    return -(-(width // 8 + 1) // 8) * 8


def halves(value):
    high = value.astype(BF16)
    return high, (value - high.astype(F32)).astype(BF16)


def dot(left, right, dims=NN):
    return lax.dot_general(left, right, dims, preferred_element_type=F32)


def iota(shape, dim):
    return lax.broadcasted_iota(jnp.int32, shape, dim)


def split_index(value, size):
    if size & (size - 1) == 0:
        return value >> (size.bit_length() - 1), value & (size - 1)
    return value // size, value % size


def rate_of(vel, grad, lap):
    strain = grad[0][0] * grad[0][0] + grad[1][1] * grad[1][1] + grad[2][2] * grad[2][2]
    strain = 2.0 * strain + 1e-06
    for one, two in ((0, 1), (0, 2), (1, 2)):
        both = grad[one][two] + grad[two][one]
        strain = strain + both * both
    eddy = viscosity + smagorinsky * (strain * lax.rsqrt(strain))
    return [
        eddy * lap[c] - (vel[0] * grad[0][c] + vel[1] * grad[1][c] + vel[2] * grad[2][c])
        for c in range(3)
    ]


def step_kernel(
    across,
    along,
    sec_hbm,
    rotor_hbm,
    entry_hbm,
    count_ref,
    mortar_hbm,
    ops_hbm,
    face_hbm,
    start_hbm,
    pre_ref,
    start_ref,
    sec_ref,
    rotor_ref,
    entry_ref,
    mortar_ref,
    ops_ref,
    face_ref,
    load_sem,
    sec_sem,
    table_ref,
    lefts_ref,
    spread_ref,
    weight_ref,
    chosen_ref,
    split_ref,
    small_ref,
    side_ref,
    thin_ref,
    yz_ref,
    x_ref,
    merged_ref,
    edge_ref,
    edge_in_ref,
    row_ref,
    row_in_ref,
    panel_sem,
    edge_send,
    edge_recv,
    row_send,
    row_recv,
):
    _, depth, height, width = sec_ref.shape
    layers, tall = depth // 8, height // 8
    plane = 8 * height
    columns = layers * tall * width
    slots = rotor_ref.shape[1]
    packed = slots // 2
    shift = packed.bit_length() - 1
    entries = entry_ref.shape[2]
    pairs = entries // 2
    blocks = mortar_ref.shape[0]
    lanes_x = width // 8
    rows = face_rows(width)
    gx = lax.axis_index("gx")
    gy = lax.axis_index("gy")
    has_x = (gx > 0, gx < across - 1)
    has_y = (gy > 0, gy < along - 1)

    def number(flag):
        return jnp.where(flag, 1, 0)

    group = 2 if layers % 2 == 0 else 1
    groups = layers // group
    scale = 2.0 / 3.0 * time_step

    def sec_load(at):
        span = pl.ds(pl.multiple_of(at * group * 8, 8), group * 8)
        return pltpu.make_async_copy(sec_hbm.at[:, span], sec_ref.at[:, span], sec_sem.at[at])

    def load(at, source, target):
        return pltpu.make_async_copy(source, target, load_sem.at[at])

    face_load = load(0, face_hbm, face_ref)
    ops_load = load(1, ops_hbm, ops_ref)
    rotor_load = load(2, rotor_hbm, rotor_ref)
    entry_load = load(0, entry_hbm, entry_ref)
    mortar_load = load(1, mortar_hbm, mortar_ref)
    start_load = load(2, start_hbm, start_ref)
    face_load.start()
    for at in range(groups):
        sec_load(at).start()
    ops_load.start()
    rotor_load.start()

    barrier = pltpu.get_barrier_semaphore()
    for d in range(1, across):
        pl.semaphore_signal(
            barrier, inc=1, device_id={"gx": lax.rem(gx + d, across)}, device_id_type=MESH
        )
    for b in range(2):
        for dx in (-1, 0, 1):
            there = has_y[b] if dx == 0 else has_y[b] & has_x[(dx + 1) // 2]

            @pl.when(there)
            def _(b=b, dx=dx):
                pl.semaphore_signal(
                    barrier,
                    inc=1,
                    device_id={"gx": gx + dx, "gy": gy + 2 * b - 1},
                    device_id_type=MESH,
                )

    def tripled(left_ref, span, size):
        high = left_ref[span, pl.ds(0, size)]
        return jnp.concatenate([high, high, left_ref[span, pl.ds(size, size)]], 1)

    line = layers * lanes_x
    face_load.wait()
    for at in range(groups):
        if at == 0:
            sec_load(at).wait()
        if at == min(1, groups - 1):
            for later in range(1, groups):
                sec_load(later).wait()
            ops_load.wait()
            rotor_load.wait()
            entry_load.start()
            mortar_load.start()
            start_load.start()
        for c in range(3):
            both = []
            for q in range(group):
                stack = sec_ref[c, pl.ds((at * group + q) * 8, 8)]
                value = jnp.concatenate(
                    [stack[:, 8 * j : 8 * j + 8].reshape(64, width) for j in range(tall)], 0
                )
                high, low = halves(value)
                split_ref[c, at * group + q, :, pl.ds(0, width)] = high
                split_ref[c, at * group + q, :, pl.ds(width, width)] = low
                both.append(jnp.concatenate([high, low, high], 1))
            small_ref[c, at] = dot(
                tripled(face_ref, slice(None), width), jnp.concatenate(both, 0), NT
            )
    square = iota((slots, slots), 0) == iota((slots, slots), 1)
    faces = jnp.broadcast_to(rotor_ref[...].astype(F32), (slots, slots))
    faces = jnp.sum(jnp.where(square, faces, 0.0), axis=1, keepdims=True).astype(jnp.int32)
    rest, face_x = split_index(faces, lanes_x)
    face_z, face_y = split_index(rest, tall)
    target = face_z * lanes_x + face_x
    pick = iota((slots, 2 * line), 1)
    pick = jnp.where((pick == target) | (pick == target + line), 1.0, 0.0).astype(BF16)

    def small_rows(c, k, first, count):
        return small_ref[c, k // group, pl.ds(first, count), pl.ds(k % group * plane, plane)]

    parts = []
    for kind in range(3):
        for c in range(3):
            high, low = halves(
                jnp.concatenate(
                    [small_rows(c, k, kind * rows, lanes_x) for k in range(layers)], 0
                )
            )
            parts.append(jnp.concatenate([high, low], 0))
            thin_ref[kind, c, pl.ds(slots, 16)] = jnp.zeros((16, plane), F32)
            for a in range(2):
                for k in range(layers):
                    thin_ref[kind, c, pl.ds(slots + 8 * a + k, 1)] = small_rows(
                        c, k, kind * rows + a * lanes_x, 1
                    )
    found = dot(pick, jnp.concatenate(parts, 1))
    for kind in range(3):
        for c in range(3):
            at = (kind * 3 + c) * plane
            thin_ref[kind, c, pl.ds(0, slots)] = found[:, at : at + plane]
    left = tripled(ops_ref, pl.ds(0, 3 * plane), plane)
    high, low = halves(jnp.concatenate([thin_ref[0, c] for c in range(3)], 0))
    side_ref[...] = dot(jnp.concatenate([high, low, high], 1), left, NT)
    thin = slots + 16
    own_half = iota((slots, plane), 1) >> 6 == face_y
    grad = [
        [thin_ref[1, c] for c in range(3)],
        [side_ref[pl.ds(c * thin, thin), pl.ds(0, plane)] for c in range(3)],
        [side_ref[pl.ds(c * thin, thin), pl.ds(plane, plane)] for c in range(3)],
    ]
    lap = [
        thin_ref[2, c] + side_ref[pl.ds(c * thin, thin), pl.ds(2 * plane, plane)]
        for c in range(3)
    ]
    for c, rate in enumerate(rate_of([thin_ref[0, c] for c in range(3)], grad, lap)):
        value = jnp.where(own_half, rate[:slots], 0.0)
        value = value + pltpu.roll(value, 64, 1)
        table_ref[gx, c] = jnp.where(
            iota((packed, plane), 1) < 64, value[:packed], value[packed:]
        )
        edge_ref[0, c] = rate[slots : slots + 8]
        edge_ref[1, c] = rate[slots + 8 :]
    e_y = iota((8, 128), 1) & 7
    for a in range(2):
        corner = edge_ref[a, 0]
        for c in (1, 2):
            corner = jnp.where(e_y == 7 - c, pltpu.roll(edge_ref[a, c], 128 - c, 1), corner)
            corner = jnp.where(e_y == c, pltpu.roll(edge_ref[a, c], c, 1), corner)
        edge_ref[a, 3] = corner

    expected = across - 1
    for b in range(2):
        expected = expected + number(has_y[b]) * (1 + number(has_x[0]) + number(has_x[1]))
    pl.semaphore_wait(barrier, expected)

    def edge_copy(a, dy):
        if dy == 0:
            source, target = edge_ref.at[a, pl.ds(0, 3)], edge_in_ref.at[1 - a, pl.ds(0, 3)]
        else:
            source, target = edge_ref.at[a, 3], edge_in_ref.at[1 - a, 3 + (1 - dy) // 2]
        return pltpu.make_async_remote_copy(
            src_ref=source,
            dst_ref=target,
            send_sem=edge_send.at[a],
            recv_sem=edge_recv.at[1 - a],
            device_id={"gx": gx + 2 * a - 1, "gy": gy + dy},
            device_id_type=MESH,
        )

    def edge_there(a, dy):
        return has_x[a] if dy == 0 else has_x[a] & has_y[(dy + 1) // 2]

    edge_list = [(a, dy) for a in range(2) for dy in (-1, 0, 1)]
    for a, dy in edge_list:

        @pl.when(edge_there(a, dy))
        def _(a=a, dy=dy):
            edge_copy(a, dy).start()

        @pl.when(jnp.logical_not(edge_there(a, dy)))
        def _(a=a, dy=dy):
            if dy == 0:
                edge_in_ref[a, pl.ds(0, 3)] = jnp.zeros((3, 8, 128), F32)
            else:
                edge_in_ref[a, 3 + (1 + dy) // 2] = jnp.zeros((8, 128), F32)

    def partner(d):
        if across & (across - 1):
            return lax.rem(gx + d, across)
        there = gx
        for bit in range(across.bit_length() - 1):
            if d >> bit & 1:
                there = there + (1 << bit) * (1 - 2 * (gx // (1 << bit) % 2))
        return there

    for d in sorted(range(1, across), key=lambda d: (-(d >> 1).bit_count(), d & 1, d)):
        pltpu.make_async_remote_copy(
            src_ref=table_ref.at[gx],
            dst_ref=table_ref.at[gx],
            send_sem=panel_sem.at[0],
            recv_sem=panel_sem.at[1],
            device_id={"gx": partner(d)},
            device_id_type=MESH,
        ).start()

    lane = iota((8, width), 1)
    y_at = iota((8, width), 0)
    y8 = lane & 7
    own = jnp.where((y8 == 0) | (y8 == 7), 0.5, 1.0)
    own = jnp.where((lane == 0) & jnp.logical_not(has_x[0]), 1.0, own)
    own = jnp.where((lane == width - 1) & jnp.logical_not(has_x[1]), 1.0, own)
    other = jnp.where(((y8 == 0) & (lane > 0)) | ((y8 == 7) & (lane < width - 1)), 0.5, 0.0)

    def row_copy(b, at):
        return pltpu.make_async_remote_copy(
            src_ref=row_ref.at[b, at],
            dst_ref=row_in_ref.at[1 - b, at],
            send_sem=row_send.at[b],
            recv_sem=row_recv.at[1 - b],
            device_id={"gy": gy + 2 * b - 1},
            device_id_type=MESH,
        )

    def product(at, kind, c):
        pieces = [split_ref[c, at * group + q] for q in range(group)]
        if kind == 0:
            high = ops_ref[pl.ds(3 * plane, width)]
            right = jnp.concatenate([high, high, ops_ref[pl.ds(3 * plane + width, width)]], 0)
            wide = jnp.concatenate(pieces, 0)
            high, low = wide[:, :width], wide[:, width:]
            x_ref[at, c] = dot(jnp.concatenate([high, low, high], 1), right)
        else:
            high = jnp.concatenate([piece[:, :width] for piece in pieces], 1)
            low = jnp.concatenate([piece[:, width:] for piece in pieces], 1)
            right = jnp.concatenate([high, low, high], 0)
            for part in range(3):
                span = pl.ds(part * plane, plane)
                yz_ref[at, c, span] = dot(tripled(ops_ref, span, plane), right)

    def layer_group(at, beside):
        steps = 8 * group
        given = 0
        for q in range(group):
            lanes = pl.ds(q * width, width)
            for z in range(8):
                while given * steps < (q * 8 + z + 1) * len(beside):
                    product(*beside[given])
                    given += 1
                z_at = (at * group + q) * 8 + z
                found = []
                for j in range(tall):
                    spot = j * 64 + 8 * z
                    x_rows = pl.ds(q * plane + spot, 8)
                    vel = [sec_ref[c, z_at, pl.ds(8 * j, 8)] for c in range(3)]
                    grad, lap = [[], [], []], []
                    for c in range(3):
                        grad[0].append(x_ref[at, c, x_rows, pl.ds(0, width)])
                        grad[1].append(yz_ref[at, c, pl.ds(spot, 8), lanes])
                        grad[2].append(yz_ref[at, c, pl.ds(plane + spot, 8), lanes])
                        lap.append(
                            x_ref[at, c, x_rows, pl.ds(width, width)]
                            + yz_ref[at, c, pl.ds(2 * plane + spot, 8), lanes]
                        )
                    merged = []
                    for rate in rate_of(vel, grad, lap):
                        partner = jnp.where(
                            y8 == 0, pltpu.roll(rate, 1, 1), pltpu.roll(rate, width - 1, 1)
                        )
                        merged.append(own * rate + other * partner)
                    found.append(merged)
                for c in range(3):
                    at_row = (c * depth + z_at) * height
                    row_ref[0, at, c, pl.ds(q * 8 + z, 1)] = found[0][c][0:1]
                    row_ref[1, at, c, pl.ds(q * 8 + z, 1)] = found[tall - 1][c][7:8]
                    for j in range(tall):
                        merged_ref[pl.ds(at_row + 8 * j, 8), :] = found[j][c]
                    for j in range(1, tall):
                        mean = 0.5 * (found[j - 1][c] + pltpu.roll(found[j][c], 7, 0))
                        merged_ref[pl.ds(at_row + 8 * j - 1, 1), :] = mean[7:8]
                        merged_ref[pl.ds(at_row + 8 * j, 1), :] = mean[7:8]
        for b in range(2):

            @pl.when(has_y[b])
            def _(b=b):
                row_copy(b, at).start()

    batches = [[(at, kind, c) for c in range(3) for kind in range(2)] for at in range(groups)]
    for item in batches[0]:
        product(*item)
    for at in range(groups):
        layer_group(at, batches[at + 1] if at + 1 < groups else [])

    entry_load.wait()
    mortar_load.wait()
    start_load.wait()

    for c in range(3):
        for k in range(1, layers):
            top = pl.ds((c * depth + 8 * k - 1) * height, height)
            bottom = pl.ds((c * depth + 8 * k) * height, height)
            mean = 0.5 * (merged_ref[top, :] + merged_ref[bottom, :])
            merged_ref[top, :] = mean
            merged_ref[bottom, :] = mean

    entry_lane = iota((pairs, entries), 1)
    entry_row = 2 * iota((pairs, entries), 0)

    def upright(kind, odd_one):
        values = jnp.broadcast_to(entry_ref[kind].astype(F32), (pairs, entries))
        values = jnp.where(entry_lane == entry_row + odd_one, values, 0.0)
        return jnp.sum(values, axis=1, keepdims=True).astype(jnp.int32)

    live = 2 * iota((pairs, 1), 0) < count_ref[0, 0]
    stator = jnp.where(live, 8 * upright(0, 0), -1)
    spread = jnp.where(iota((pairs, columns), 1) == stator, 0.5, 0.0)
    factor = 1.0 - jnp.max(spread, axis=0, keepdims=True)
    spread_ref[pl.ds(0, pairs), :] = spread.astype(BF16)
    spread_ref[pl.ds(pairs, pairs), :] = spread.astype(BF16)
    row_e = iota((128, 1), 0)
    layer_e = row_e & 7
    side_e = (row_e >> 4) & 1
    tall_e = row_e >> 5
    kept = (tall_e < tall) & (layer_e < layers)
    kept = kept & (jnp.where(side_e == 0, number(has_x[0]), number(has_x[1])) > 0)
    to_e = jnp.where(kept, (layer_e * tall + tall_e) * width + side_e * (width - 1), -1)
    spread_ref[pl.ds(2 * pairs, 128), :] = jnp.where(
        iota((128, columns), 1) == to_e, 0.5 * factor, 0.0
    ).astype(BF16)

    for k in range(layers):
        for j in range(tall):
            at = (k * tall + j) * width
            keep = jnp.broadcast_to(scale * factor[:, at : at + width], (8, width))
            if j == 0:
                keep = jnp.where((y_at == 0) & has_y[0], 0.5 * keep, keep)
            if j == tall - 1:
                keep = jnp.where((y_at == 7) & has_y[1], 0.5 * keep, keep)
            for c in range(3):
                for z in range(8 * k, 8 * k + 8):
                    spot = pl.ds((c * depth + z) * height + 8 * j, 8)
                    pre_ref[spot, :] = (
                        start_ref[c, z, pl.ds(8 * j, 8)] * (1.0 / 3.0)
                        + sec_ref[c, z, pl.ds(8 * j, 8)] * (2.0 / 3.0)
                        + merged_ref[spot, :] * keep
                    )

    for b in range(blocks):
        high, low = halves(scale * mortar_ref[b])
        weight_ref[pl.ds(64 * b, 64)] = jnp.concatenate(
            [high, high, low, jnp.zeros((64, 64), BF16)], 1
        )

    lane_half = iota((pairs, 128), 1) >> 6
    for odd_one in (0, 1):
        chosen = jnp.where(live, upright(2, odd_one), -1)
        for p in range(blocks // 2):
            chosen_ref[pl.ds(odd_one * pairs, pairs), pl.ds(p * 128, 128)] = jnp.where(
                chosen == lane_half + 2 * p, 1.0, 0.0
            )
    source = jnp.concatenate([upright(1, 0), upright(1, 1)], 0)
    spots = across * packed
    table_row = iota((2 * pairs, spots), 1)
    first_id = table_row + ((table_row >> shift) << shift)
    gather = jnp.where((source == first_id) | (source == first_id + packed), 1.0, 0.0).astype(BF16)
    source_half = (source >> shift) & 1
    straight = iota((2 * pairs, 128), 1) >> 6 == source_half
    take = jnp.where((iota((64, 128), 1) & 63) == iota((64, 128), 0), 1.0, 0.0).astype(BF16)

    e_lane = iota((8, 128), 1)
    e_row = iota((8, 128), 0)
    e_y = e_lane & 7
    e_z = (e_lane >> 3) & 7
    e_low = e_lane < 64
    many = 1 + number(has_y[0]) + number(has_y[1])
    for a in range(2):
        for n in range(1, 4):

            @pl.when(has_x[a] & (many == n))
            def _(a=a, n=n):
                came = edge_in_ref.at[a, pl.ds(0, 2 + n)]
                pltpu.make_async_remote_copy(
                    src_ref=came,
                    dst_ref=came,
                    send_sem=edge_send.at[a],
                    recv_sem=edge_recv.at[a],
                    device_id={"gx": gx + 2 * a - 1},
                    device_id_type=MESH,
                ).wait()

    y_move = ((e_y == 0) & (jnp.logical_not(e_low) | has_y[0])) | (
        (e_y == 7) & (e_low | has_y[1])
    )
    z_move = ((e_z == 0) & (e_row > 0)) | ((e_z == 7) & (e_row < layers - 1))
    for c in range(3):
        stack = []
        for a in range(2):
            mid = edge_in_ref[a, c]
            near = jnp.where(
                e_y == 0,
                jnp.where(e_low, pltpu.roll(edge_in_ref[a, 3], 57 + c, 1), pltpu.roll(mid, 57, 1)),
                jnp.where(e_low, pltpu.roll(mid, 71, 1), pltpu.roll(edge_in_ref[a, 4], 71 - c, 1)),
            )
            mid = jnp.where(y_move, 0.5 * (mid + near), mid)
            near = jnp.where(
                e_z == 0,
                pltpu.roll(pltpu.roll(mid, 72, 1), 1, 0),
                pltpu.roll(pltpu.roll(mid, 56, 1), 7, 0),
            )
            mid = scale * jnp.where(z_move, 0.5 * (mid + near), mid)
            top = mid.astype(BF16).astype(F32)
            stack += [top, mid - top]
        stack = jnp.concatenate(stack, 0)
        low_stack = iota(stack.shape, 1) < 64
        stack = jnp.concatenate(
            [
                jnp.where(low_stack, stack, 0.0),
                jnp.where(low_stack, 0.0, stack),
                jnp.zeros((64, 128), F32),
            ],
            0,
        )
        lefts_ref[pl.ds(64 * c, 64), pl.ds(entries, 128)] = dot(
            take, stack.astype(BF16), NT
        ).astype(BF16)

    came = table_ref.at[pl.ds(0, across - 1)]
    pltpu.make_async_remote_copy(
        src_ref=came,
        dst_ref=came,
        send_sem=panel_sem.at[0],
        recv_sem=panel_sem.at[1],
        device_id={"gx": lax.rem(gx + 1, across)},
        device_id_type=MESH,
    ).wait()
    table = jnp.concatenate([table_ref[:, c].reshape(spots, 128) for c in range(3)], 1)
    high, low = halves(table)
    incoming = dot(jnp.concatenate([gather, gather], 1), jnp.concatenate([high, low], 0))
    low_lane = iota((entries, 128), 1) < 64
    spaced = []
    for c in range(3):
        part = incoming[:, c * 128 : c * 128 + 128]
        part = jnp.where(straight, part, pltpu.roll(part, 64, 1))
        top = part.astype(BF16).astype(F32)
        spaced.append(jnp.concatenate([jnp.where(low_lane, top, part - top), top], 1).astype(BF16))
    spaced = jnp.concatenate(spaced, 0)
    total = [0.0] * 3
    for p in range(blocks // 4):
        product = dot(spaced, weight_ref[pl.ds(256 * p, 256)], NT)
        for half in range(2):
            mask = chosen_ref[:, pl.ds(256 * p + 128 * half, 128)]
            for c in range(3):
                total[c] = total[c] + mask * product[
                    c * entries : (c + 1) * entries, 128 * half : 128 * half + 128
                ]
    stack = []
    for c in range(3):
        value = total[c][:pairs] + total[c][pairs:]
        value = value + pltpu.roll(value, 64, 1)
        top = value.astype(BF16).astype(F32)
        stack += [top, value - top]
    stack = jnp.concatenate(stack, 0).astype(BF16)
    take = jnp.where(iota((64, 128), 1) == iota((64, 128), 0), 1.0, 0.0).astype(BF16)
    turned = dot(take, stack, NT).astype(BF16)
    for c in range(3):
        lefts_ref[pl.ds(64 * c, 64), pl.ds(0, entries)] = turned[:, c * entries : (c + 1) * entries]

    for k in range(layers):
        change = dot(lefts_ref[...], spread_ref[:, pl.ds(k * tall * width, tall * width)])
        for c in range(3):
            for j in range(tall):
                for z in range(8):
                    spot = pl.ds((c * depth + 8 * k + z) * height + 8 * j, 8)
                    row = 64 * c + 8 * z
                    pre_ref[spot, :] = (
                        pre_ref[spot, :] + change[row : row + 8, j * width : j * width + width]
                    )

    z_at = iota((depth, width), 0)
    z8 = z_at & 7
    z_low = (z8 == 0) & (z_at > 0)
    z_high = (z8 == 7) & (z_at < depth - 1)
    for b in range(2):

        @pl.when(has_y[b])
        def _(b=b):
            pltpu.make_async_remote_copy(
                src_ref=row_ref.at[b],
                dst_ref=row_in_ref.at[b],
                send_sem=row_send.at[b],
                recv_sem=row_recv.at[b],
                device_id={"gy": gy + 2 * b - 1},
                device_id_type=MESH,
            ).wait()
            j = b * (tall - 1)
            keep = jnp.concatenate(
                [
                    jnp.broadcast_to(
                        0.5 * scale * factor[:, (k * tall + j) * width : (k * tall + j + 1) * width],
                        (8, width),
                    )
                    for k in range(layers)
                ],
                0,
            )
            for c in range(3):
                value = jnp.concatenate([row_in_ref[b, at, c] for at in range(groups)], 0)
                near = jnp.where(
                    z_low, pltpu.roll(value, 1, 0), pltpu.roll(value, depth - 1, 0)
                )
                value = jnp.where(z_low | z_high, 0.5 * (value + near), value)
                spot = (pl.ds(c * depth * height + b * (height - 1), depth, stride=height), slice(None))
                pre_ref[spot] = pre_ref[spot] + keep * value


def finish_kernel(pre_ref, out_hbm, out_sem):
    for c in range(3):
        pltpu.make_async_copy(pre_ref.at[c], out_hbm.at[c], out_sem).start()
    pltpu.make_async_copy(pre_ref, out_hbm, out_sem).wait()


def local(initial, sectioned, rotor_faces, intersections, live_counts, mortar_blocks):
    across = lax.axis_size("gx")
    along = lax.axis_size("gy")
    _, depth, height, width = sectioned.shape
    ops, face = operators(height, width)
    plane = 8 * height
    layers = depth // 8
    columns = layers * (height // 8) * width
    group = 2 if layers % 2 == 0 else 1
    groups = layers // group
    packed = rotor_faces.shape[1] // 2
    entries = intersections.shape[1]
    blocks = mortar_blocks.shape[0]
    room = 4 * int(np.prod(sectioned.shape))
    hbm, vmem = pl.BlockSpec(memory_space=pltpu.HBM), pl.BlockSpec(memory_space=pltpu.VMEM)
    staged = pl.pallas_call(
        functools.partial(step_kernel, across, along),
        out_shape=pltpu.VMEM((3 * depth * height, width), F32),
        in_specs=[hbm] * 3 + [pl.BlockSpec(memory_space=pltpu.SMEM)] + [hbm] * 4,
        out_specs=vmem,
        scratch_shapes=[
            pltpu.VMEM(initial.shape, F32),
            pltpu.VMEM(sectioned.shape, F32),
            pltpu.VMEM(rotor_faces.shape, jnp.int32),
            pltpu.VMEM((3, 1, entries), jnp.int32),
            pltpu.VMEM(mortar_blocks.shape, F32),
            pltpu.VMEM(ops.shape, BF16),
            pltpu.VMEM(face.shape, BF16),
            pltpu.SemaphoreType.DMA((3,)),
            pltpu.SemaphoreType.DMA((groups,)),
            pltpu.VMEM((across, 3, packed, 128), F32),
            pltpu.VMEM((3 * 64, entries + 128), BF16),
            pltpu.VMEM((entries + 128, columns), BF16),
            pltpu.VMEM((64 * blocks, 256), BF16),
            pltpu.VMEM((entries, 64 * blocks), F32),
            pltpu.VMEM((3, layers, plane, 2 * width), BF16),
            pltpu.VMEM((3, groups, face.shape[0], group * plane), F32),
            pltpu.VMEM((3 * (rotor_faces.shape[1] + 16), 3 * plane), F32),
            pltpu.VMEM((3, 3, rotor_faces.shape[1] + 16, plane), F32),
            pltpu.VMEM((groups, 3, 3 * plane, group * width), F32),
            pltpu.VMEM((groups, 3, group * plane, 2 * width), F32),
            pltpu.VMEM((3 * depth * height, width), F32),
            pltpu.VMEM((2, 4, 8, 128), F32),
            pltpu.VMEM((2, 5, 8, 128), F32),
            pltpu.VMEM((2, groups, 3, group * 8, width), F32),
            pltpu.VMEM((2, groups, 3, group * 8, width), F32),
            pltpu.SemaphoreType.DMA((2,)),
            pltpu.SemaphoreType.DMA((2,)),
            pltpu.SemaphoreType.DMA((2,)),
            pltpu.SemaphoreType.DMA((2,)),
            pltpu.SemaphoreType.DMA((2,)),
        ],
        compiler_params=pltpu.CompilerParams(
            collective_id=0, has_side_effects=True, vmem_limit_bytes=67043328 - room
        ),
        name="step",
    )(
        sectioned,
        rotor_faces,
        jnp.transpose(intersections, (2, 0, 1)),
        live_counts,
        mortar_blocks,
        jnp.asarray(ops),
        jnp.asarray(face),
        initial,
    )
    return pl.pallas_call(
        finish_kernel,
        out_shape=jax.ShapeDtypeStruct(sectioned.shape, F32),
        in_specs=[vmem],
        out_specs=hbm,
        scratch_shapes=[pltpu.SemaphoreType.DMA],
        compiler_params=pltpu.CompilerParams(vmem_limit_bytes=32 * 1024 * 1024),
        name="finish",
    )(staged.reshape(sectioned.shape))


def solution(mesh):
    return jax.shard_map(
        local,
        mesh=mesh,
        in_specs=(
            P(None, None, "gy", "gx"),
            P(None, None, "gy", "gx"),
            P("gy", "gx"),
            P("gy", "gx", None),
            P("gy", "gx"),
            P(),
        ),
        out_specs=P(None, None, "gy", "gx"),
        check_vma=False,
    )
```

```python
import functools

import jax
import jax.numpy as jnp
import numpy as np
from jax import lax
from jax.experimental import pallas as pl
from jax.experimental.pallas import tpu as pltpu
from jax.sharding import PartitionSpec as P

time_step = 0.02
viscosity = 0.005
smagorinsky = 0.002
gll_interior = [
    -0.8717401485096066,
    -0.5917001814331423,
    -0.2092992179024789,
    0.2092992179024789,
    0.5917001814331423,
    0.8717401485096066,
]


def legendre_seven(points):
    lower_poly = points * 0.0 + 1.0
    current = points * 1.0
    for order_at in range(1, 7):
        following = ((2 * order_at + 1) * points * current - order_at * lower_poly) / (order_at + 1)
        lower_poly = current
        current = following
    return current


def gll_tables():
    degree = 7
    points = np.array([-1.0] + gll_interior + [1.0])
    values = legendre_seven(points)
    slope_table = np.zeros((degree + 1, degree + 1))
    for row_at in range(degree + 1):
        for col_at in range(degree + 1):
            if row_at != col_at:
                slope_table[row_at, col_at] = values[row_at] / (
                    values[col_at] * (points[row_at] - points[col_at])
                )
    slope_table[0, 0] = -degree * (degree + 1) / 4.0
    slope_table[degree, degree] = degree * (degree + 1) / 4.0
    return (slope_table, slope_table @ slope_table)


F32 = jnp.float32
BF16 = jnp.bfloat16
MESH = pl.DeviceIdType.MESH
NT = (((1,), (1,)), ((), ()))
NN = (((1,), (0,)), ((), ()))


def split_table(table):
    table = np.asarray(table, np.float32)
    high = table.astype(BF16)
    return high, (table - high.astype(np.float32)).astype(BF16)


def operators(height, width):
    slope, curve = gll_tables()
    tall = np.eye(height // 8)
    eye = np.eye(8)
    left = np.concatenate(
        [
            np.kron(tall, np.kron(eye, slope)),
            np.kron(tall, np.kron(slope, eye)),
            np.kron(tall, np.kron(eye, curve) + np.kron(curve, eye)),
        ]
    )
    left = np.concatenate(split_table(left), 1)
    cols = np.eye(width // 8)
    along, twice = np.kron(cols, slope), np.kron(cols, curve)
    right = np.concatenate(split_table(np.concatenate([along.T, twice.T], 1)), 0)
    rows = face_rows(width)
    nodes = list(range(0, width, 8)) + [width - 1]
    face = np.zeros((-(-3 * rows // 16) * 16, width))
    for at, table in enumerate([np.eye(width), along, twice]):
        face[at * rows : at * rows + len(nodes)] = table[nodes]
    return np.concatenate([left, right], 0), np.concatenate(split_table(face), 1)


def face_rows(width):
    return -(-(width // 8 + 1) // 8) * 8


def halves(value):
    high = value.astype(BF16)
    return high, (value - high.astype(F32)).astype(BF16)


def dot(left, right, dims=NN):
    return lax.dot_general(left, right, dims, preferred_element_type=F32)


def iota(shape, dim):
    return lax.broadcasted_iota(jnp.int32, shape, dim)


def split_index(value, size):
    if size & (size - 1) == 0:
        return value >> (size.bit_length() - 1), value & (size - 1)
    return value // size, value % size


def rate_of(vel, grad, lap):
    strain = grad[0][0] * grad[0][0] + grad[1][1] * grad[1][1] + grad[2][2] * grad[2][2]
    strain = 2.0 * strain + 1e-06
    for one, two in ((0, 1), (0, 2), (1, 2)):
        both = grad[one][two] + grad[two][one]
        strain = strain + both * both
    eddy = viscosity + smagorinsky * (strain * lax.rsqrt(strain))
    return [
        eddy * lap[c] - (vel[0] * grad[0][c] + vel[1] * grad[1][c] + vel[2] * grad[2][c])
        for c in range(3)
    ]


def step_kernel(
    across,
    along,
    sec_hbm,
    rotor_hbm,
    entry_hbm,
    count_ref,
    mortar_hbm,
    ops_hbm,
    face_hbm,
    start_hbm,
    pre_ref,
    lefts_ref,
    spread_ref,
    start_ref,
    sec_ref,
    rotor_ref,
    entry_ref,
    mortar_ref,
    ops_ref,
    face_ref,
    load_sem,
    sec_sem,
    table_ref,
    weight_ref,
    chosen_ref,
    split_ref,
    small_ref,
    side_ref,
    thin_ref,
    yz_ref,
    x_ref,
    merged_ref,
    edge_ref,
    edge_in_ref,
    row_ref,
    row_in_ref,
    panel_sem,
    edge_send,
    edge_recv,
    row_send,
    row_recv,
):
    _, depth, height, width = sec_ref.shape
    layers, tall = depth // 8, height // 8
    plane = 8 * height
    columns = layers * tall * width
    slots = rotor_ref.shape[1]
    packed = slots // 2
    shift = packed.bit_length() - 1
    entries = entry_ref.shape[2]
    pairs = entries // 2
    blocks = mortar_ref.shape[0]
    lanes_x = width // 8
    rows = face_rows(width)
    gx = lax.axis_index("gx")
    gy = lax.axis_index("gy")
    has_x = (gx > 0, gx < across - 1)
    has_y = (gy > 0, gy < along - 1)

    def number(flag):
        return jnp.where(flag, 1, 0)

    group = 2 if layers % 2 == 0 else 1
    groups = layers // group
    scale = 2.0 / 3.0 * time_step

    def sec_load(at):
        span = pl.ds(pl.multiple_of(at * group * 8, 8), group * 8)
        return pltpu.make_async_copy(sec_hbm.at[:, span], sec_ref.at[:, span], sec_sem.at[at])

    def load(at, source, target):
        return pltpu.make_async_copy(source, target, load_sem.at[at])

    face_load = load(0, face_hbm, face_ref)
    ops_load = load(1, ops_hbm, ops_ref)
    rotor_load = load(2, rotor_hbm, rotor_ref)
    entry_load = load(0, entry_hbm, entry_ref)
    mortar_load = load(1, mortar_hbm, mortar_ref)
    start_load = load(2, start_hbm, start_ref)
    face_load.start()
    for at in range(groups):
        sec_load(at).start()
    ops_load.start()
    rotor_load.start()

    barrier = pltpu.get_barrier_semaphore()
    for d in range(1, across):
        pl.semaphore_signal(
            barrier, inc=1, device_id={"gx": lax.rem(gx + d, across)}, device_id_type=MESH
        )
    for b in range(2):
        for dx in (-1, 0, 1):
            there = has_y[b] if dx == 0 else has_y[b] & has_x[(dx + 1) // 2]

            @pl.when(there)
            def _(b=b, dx=dx):
                pl.semaphore_signal(
                    barrier,
                    inc=1,
                    device_id={"gx": gx + dx, "gy": gy + 2 * b - 1},
                    device_id_type=MESH,
                )

    def tripled(left_ref, span, size):
        high = left_ref[span, pl.ds(0, size)]
        return jnp.concatenate([high, high, left_ref[span, pl.ds(size, size)]], 1)

    line = layers * lanes_x
    face_load.wait()
    for at in range(groups):
        if at == 0:
            sec_load(at).wait()
        if at == min(1, groups - 1):
            for later in range(1, groups):
                sec_load(later).wait()
            ops_load.wait()
            rotor_load.wait()
            entry_load.start()
            mortar_load.start()
            start_load.start()
        for c in range(3):
            both = []
            for q in range(group):
                stack = sec_ref[c, pl.ds((at * group + q) * 8, 8)]
                value = jnp.concatenate(
                    [stack[:, 8 * j : 8 * j + 8].reshape(64, width) for j in range(tall)], 0
                )
                high, low = halves(value)
                split_ref[c, at * group + q, :, pl.ds(0, width)] = high
                split_ref[c, at * group + q, :, pl.ds(width, width)] = low
                both.append(jnp.concatenate([high, low, high], 1))
            small_ref[c, at] = dot(
                tripled(face_ref, slice(None), width), jnp.concatenate(both, 0), NT
            )
    square = iota((slots, slots), 0) == iota((slots, slots), 1)
    faces = jnp.broadcast_to(rotor_ref[...].astype(F32), (slots, slots))
    faces = jnp.sum(jnp.where(square, faces, 0.0), axis=1, keepdims=True).astype(jnp.int32)
    rest, face_x = split_index(faces, lanes_x)
    face_z, face_y = split_index(rest, tall)
    target = face_z * lanes_x + face_x
    pick = iota((slots, 2 * line), 1)
    pick = jnp.where((pick == target) | (pick == target + line), 1.0, 0.0).astype(BF16)

    def small_rows(c, k, first, count):
        return small_ref[c, k // group, pl.ds(first, count), pl.ds(k % group * plane, plane)]

    parts = []
    for kind in range(3):
        for c in range(3):
            high, low = halves(
                jnp.concatenate(
                    [small_rows(c, k, kind * rows, lanes_x) for k in range(layers)], 0
                )
            )
            parts.append(jnp.concatenate([high, low], 0))
            thin_ref[kind, c, pl.ds(slots, 16)] = jnp.zeros((16, plane), F32)
            for a in range(2):
                for k in range(layers):
                    thin_ref[kind, c, pl.ds(slots + 8 * a + k, 1)] = small_rows(
                        c, k, kind * rows + a * lanes_x, 1
                    )
    found = dot(pick, jnp.concatenate(parts, 1))
    for kind in range(3):
        for c in range(3):
            at = (kind * 3 + c) * plane
            thin_ref[kind, c, pl.ds(0, slots)] = found[:, at : at + plane]
    left = tripled(ops_ref, pl.ds(0, 3 * plane), plane)
    high, low = halves(jnp.concatenate([thin_ref[0, c] for c in range(3)], 0))
    side_ref[...] = dot(jnp.concatenate([high, low, high], 1), left, NT)
    thin = slots + 16
    own_half = iota((slots, plane), 1) >> 6 == face_y
    grad = [
        [thin_ref[1, c] for c in range(3)],
        [side_ref[pl.ds(c * thin, thin), pl.ds(0, plane)] for c in range(3)],
        [side_ref[pl.ds(c * thin, thin), pl.ds(plane, plane)] for c in range(3)],
    ]
    lap = [
        thin_ref[2, c] + side_ref[pl.ds(c * thin, thin), pl.ds(2 * plane, plane)]
        for c in range(3)
    ]
    for c, rate in enumerate(rate_of([thin_ref[0, c] for c in range(3)], grad, lap)):
        value = jnp.where(own_half, rate[:slots], 0.0)
        value = value + pltpu.roll(value, 64, 1)
        table_ref[gx, c] = jnp.where(
            iota((packed, plane), 1) < 64, value[:packed], value[packed:]
        )
        edge_ref[0, c] = rate[slots : slots + 8]
        edge_ref[1, c] = rate[slots + 8 :]
    e_y = iota((8, 128), 1) & 7
    for a in range(2):
        corner = edge_ref[a, 0]
        for c in (1, 2):
            corner = jnp.where(e_y == 7 - c, pltpu.roll(edge_ref[a, c], 128 - c, 1), corner)
            corner = jnp.where(e_y == c, pltpu.roll(edge_ref[a, c], c, 1), corner)
        edge_ref[a, 3] = corner

    expected = across - 1
    for b in range(2):
        expected = expected + number(has_y[b]) * (1 + number(has_x[0]) + number(has_x[1]))
    pl.semaphore_wait(barrier, expected)

    def edge_copy(a, dy):
        if dy == 0:
            source, target = edge_ref.at[a, pl.ds(0, 3)], edge_in_ref.at[1 - a, pl.ds(0, 3)]
        else:
            source, target = edge_ref.at[a, 3], edge_in_ref.at[1 - a, 3 + (1 - dy) // 2]
        return pltpu.make_async_remote_copy(
            src_ref=source,
            dst_ref=target,
            send_sem=edge_send.at[a],
            recv_sem=edge_recv.at[1 - a],
            device_id={"gx": gx + 2 * a - 1, "gy": gy + dy},
            device_id_type=MESH,
        )

    def edge_there(a, dy):
        return has_x[a] if dy == 0 else has_x[a] & has_y[(dy + 1) // 2]

    edge_list = [(a, dy) for a in range(2) for dy in (-1, 0, 1)]
    for a, dy in edge_list:

        @pl.when(edge_there(a, dy))
        def _(a=a, dy=dy):
            edge_copy(a, dy).start()

        @pl.when(jnp.logical_not(edge_there(a, dy)))
        def _(a=a, dy=dy):
            if dy == 0:
                edge_in_ref[a, pl.ds(0, 3)] = jnp.zeros((3, 8, 128), F32)
            else:
                edge_in_ref[a, 3 + (1 + dy) // 2] = jnp.zeros((8, 128), F32)

    def partner(d):
        if across & (across - 1):
            return lax.rem(gx + d, across)
        there = gx
        for bit in range(across.bit_length() - 1):
            if d >> bit & 1:
                there = there + (1 << bit) * (1 - 2 * (gx // (1 << bit) % 2))
        return there

    for d in sorted(range(1, across), key=lambda d: (-(d >> 1).bit_count(), d & 1, d)):
        pltpu.make_async_remote_copy(
            src_ref=table_ref.at[gx],
            dst_ref=table_ref.at[gx],
            send_sem=panel_sem.at[0],
            recv_sem=panel_sem.at[1],
            device_id={"gx": partner(d)},
            device_id_type=MESH,
        ).start()

    lane = iota((8, width), 1)
    y_at = iota((8, width), 0)
    y8 = lane & 7
    own = jnp.where((y8 == 0) | (y8 == 7), 0.5, 1.0)
    own = jnp.where((lane == 0) & jnp.logical_not(has_x[0]), 1.0, own)
    own = jnp.where((lane == width - 1) & jnp.logical_not(has_x[1]), 1.0, own)
    other = jnp.where(((y8 == 0) & (lane > 0)) | ((y8 == 7) & (lane < width - 1)), 0.5, 0.0)

    def row_copy(b, at):
        return pltpu.make_async_remote_copy(
            src_ref=row_ref.at[b, at],
            dst_ref=row_in_ref.at[1 - b, at],
            send_sem=row_send.at[b],
            recv_sem=row_recv.at[1 - b],
            device_id={"gy": gy + 2 * b - 1},
            device_id_type=MESH,
        )

    def product(at, kind, c):
        pieces = [split_ref[c, at * group + q] for q in range(group)]
        if kind == 0:
            high = ops_ref[pl.ds(3 * plane, width)]
            right = jnp.concatenate([high, high, ops_ref[pl.ds(3 * plane + width, width)]], 0)
            wide = jnp.concatenate(pieces, 0)
            high, low = wide[:, :width], wide[:, width:]
            x_ref[at, c] = dot(jnp.concatenate([high, low, high], 1), right)
        else:
            high = jnp.concatenate([piece[:, :width] for piece in pieces], 1)
            low = jnp.concatenate([piece[:, width:] for piece in pieces], 1)
            right = jnp.concatenate([high, low, high], 0)
            for part in range(3):
                span = pl.ds(part * plane, plane)
                yz_ref[at, c, span] = dot(tripled(ops_ref, span, plane), right)

    def layer_group(at, beside):
        steps = 8 * group
        given = 0
        for q in range(group):
            lanes = pl.ds(q * width, width)
            for z in range(8):
                while given * steps < (q * 8 + z + 1) * len(beside):
                    product(*beside[given])
                    given += 1
                z_at = (at * group + q) * 8 + z
                found = []
                for j in range(tall):
                    spot = j * 64 + 8 * z
                    x_rows = pl.ds(q * plane + spot, 8)
                    vel = [sec_ref[c, z_at, pl.ds(8 * j, 8)] for c in range(3)]
                    grad, lap = [[], [], []], []
                    for c in range(3):
                        grad[0].append(x_ref[at, c, x_rows, pl.ds(0, width)])
                        grad[1].append(yz_ref[at, c, pl.ds(spot, 8), lanes])
                        grad[2].append(yz_ref[at, c, pl.ds(plane + spot, 8), lanes])
                        lap.append(
                            x_ref[at, c, x_rows, pl.ds(width, width)]
                            + yz_ref[at, c, pl.ds(2 * plane + spot, 8), lanes]
                        )
                    merged = []
                    for rate in rate_of(vel, grad, lap):
                        partner = jnp.where(
                            y8 == 0, pltpu.roll(rate, 1, 1), pltpu.roll(rate, width - 1, 1)
                        )
                        merged.append(own * rate + other * partner)
                    found.append(merged)
                for c in range(3):
                    at_row = (c * depth + z_at) * height
                    row_ref[0, at, c, pl.ds(q * 8 + z, 1)] = found[0][c][0:1]
                    row_ref[1, at, c, pl.ds(q * 8 + z, 1)] = found[tall - 1][c][7:8]
                    for j in range(tall):
                        merged_ref[pl.ds(at_row + 8 * j, 8), :] = found[j][c]
                    for j in range(1, tall):
                        mean = 0.5 * (found[j - 1][c] + pltpu.roll(found[j][c], 7, 0))
                        merged_ref[pl.ds(at_row + 8 * j - 1, 1), :] = mean[7:8]
                        merged_ref[pl.ds(at_row + 8 * j, 1), :] = mean[7:8]
        for b in range(2):

            @pl.when(has_y[b])
            def _(b=b):
                row_copy(b, at).start()

    batches = [[(at, kind, c) for c in range(3) for kind in range(2)] for at in range(groups)]
    for item in batches[0]:
        product(*item)
    for at in range(groups):
        layer_group(at, batches[at + 1] if at + 1 < groups else [])

    entry_load.wait()
    mortar_load.wait()
    start_load.wait()

    for c in range(3):
        for k in range(1, layers):
            top = pl.ds((c * depth + 8 * k - 1) * height, height)
            bottom = pl.ds((c * depth + 8 * k) * height, height)
            mean = 0.5 * (merged_ref[top, :] + merged_ref[bottom, :])
            merged_ref[top, :] = mean
            merged_ref[bottom, :] = mean

    entry_lane = iota((pairs, entries), 1)
    entry_row = 2 * iota((pairs, entries), 0)

    def upright(kind, odd_one):
        values = jnp.broadcast_to(entry_ref[kind].astype(F32), (pairs, entries))
        values = jnp.where(entry_lane == entry_row + odd_one, values, 0.0)
        return jnp.sum(values, axis=1, keepdims=True).astype(jnp.int32)

    live = 2 * iota((pairs, 1), 0) < count_ref[0, 0]
    stator = jnp.where(live, 8 * upright(0, 0), -1)
    spread = jnp.where(iota((pairs, columns), 1) == stator, 0.5, 0.0)
    factor = 1.0 - jnp.max(spread, axis=0, keepdims=True)
    spread_ref[pl.ds(0, pairs), :] = spread.astype(BF16)
    spread_ref[pl.ds(pairs, pairs), :] = spread.astype(BF16)
    row_e = iota((128, 1), 0)
    layer_e = row_e & 7
    side_e = (row_e >> 4) & 1
    tall_e = row_e >> 5
    kept = (tall_e < tall) & (layer_e < layers)
    kept = kept & (jnp.where(side_e == 0, number(has_x[0]), number(has_x[1])) > 0)
    to_e = jnp.where(kept, (layer_e * tall + tall_e) * width + side_e * (width - 1), -1)
    spread_ref[pl.ds(2 * pairs, 128), :] = jnp.where(
        iota((128, columns), 1) == to_e, 0.5 * factor, 0.0
    ).astype(BF16)

    for k in range(layers):
        for j in range(tall):
            at = (k * tall + j) * width
            keep = jnp.broadcast_to(scale * factor[:, at : at + width], (8, width))
            if j == 0:
                keep = jnp.where((y_at == 0) & has_y[0], 0.5 * keep, keep)
            if j == tall - 1:
                keep = jnp.where((y_at == 7) & has_y[1], 0.5 * keep, keep)
            for c in range(3):
                for z in range(8 * k, 8 * k + 8):
                    spot = pl.ds((c * depth + z) * height + 8 * j, 8)
                    pre_ref[spot, :] = (
                        start_ref[c, z, pl.ds(8 * j, 8)] * (1.0 / 3.0)
                        + sec_ref[c, z, pl.ds(8 * j, 8)] * (2.0 / 3.0)
                        + merged_ref[spot, :] * keep
                    )

    for b in range(blocks):
        high, low = halves(scale * mortar_ref[b])
        weight_ref[pl.ds(64 * b, 64)] = jnp.concatenate(
            [high, high, low, jnp.zeros((64, 64), BF16)], 1
        )

    lane_half = iota((pairs, 128), 1) >> 6
    for odd_one in (0, 1):
        chosen = jnp.where(live, upright(2, odd_one), -1)
        for p in range(blocks // 2):
            chosen_ref[pl.ds(odd_one * pairs, pairs), pl.ds(p * 128, 128)] = jnp.where(
                chosen == lane_half + 2 * p, 1.0, 0.0
            )
    source = jnp.concatenate([upright(1, 0), upright(1, 1)], 0)
    spots = across * packed
    table_row = iota((2 * pairs, spots), 1)
    first_id = table_row + ((table_row >> shift) << shift)
    gather = jnp.where((source == first_id) | (source == first_id + packed), 1.0, 0.0).astype(BF16)
    source_half = (source >> shift) & 1
    straight = iota((2 * pairs, 128), 1) >> 6 == source_half
    take = jnp.where((iota((64, 128), 1) & 63) == iota((64, 128), 0), 1.0, 0.0).astype(BF16)

    e_lane = iota((8, 128), 1)
    e_row = iota((8, 128), 0)
    e_y = e_lane & 7
    e_z = (e_lane >> 3) & 7
    e_low = e_lane < 64
    many = 1 + number(has_y[0]) + number(has_y[1])
    for a in range(2):
        for n in range(1, 4):

            @pl.when(has_x[a] & (many == n))
            def _(a=a, n=n):
                came = edge_in_ref.at[a, pl.ds(0, 2 + n)]
                pltpu.make_async_remote_copy(
                    src_ref=came,
                    dst_ref=came,
                    send_sem=edge_send.at[a],
                    recv_sem=edge_recv.at[a],
                    device_id={"gx": gx + 2 * a - 1},
                    device_id_type=MESH,
                ).wait()

    y_move = ((e_y == 0) & (jnp.logical_not(e_low) | has_y[0])) | (
        (e_y == 7) & (e_low | has_y[1])
    )
    z_move = ((e_z == 0) & (e_row > 0)) | ((e_z == 7) & (e_row < layers - 1))
    for c in range(3):
        stack = []
        for a in range(2):
            mid = edge_in_ref[a, c]
            near = jnp.where(
                e_y == 0,
                jnp.where(e_low, pltpu.roll(edge_in_ref[a, 3], 57 + c, 1), pltpu.roll(mid, 57, 1)),
                jnp.where(e_low, pltpu.roll(mid, 71, 1), pltpu.roll(edge_in_ref[a, 4], 71 - c, 1)),
            )
            mid = jnp.where(y_move, 0.5 * (mid + near), mid)
            near = jnp.where(
                e_z == 0,
                pltpu.roll(pltpu.roll(mid, 72, 1), 1, 0),
                pltpu.roll(pltpu.roll(mid, 56, 1), 7, 0),
            )
            mid = scale * jnp.where(z_move, 0.5 * (mid + near), mid)
            top = mid.astype(BF16).astype(F32)
            stack += [top, mid - top]
        stack = jnp.concatenate(stack, 0)
        low_stack = iota(stack.shape, 1) < 64
        stack = jnp.concatenate(
            [
                jnp.where(low_stack, stack, 0.0),
                jnp.where(low_stack, 0.0, stack),
                jnp.zeros((64, 128), F32),
            ],
            0,
        )
        lefts_ref[pl.ds(64 * c, 64), pl.ds(entries, 128)] = dot(
            take, stack.astype(BF16), NT
        ).astype(BF16)

    came = table_ref.at[pl.ds(0, across - 1)]
    pltpu.make_async_remote_copy(
        src_ref=came,
        dst_ref=came,
        send_sem=panel_sem.at[0],
        recv_sem=panel_sem.at[1],
        device_id={"gx": lax.rem(gx + 1, across)},
        device_id_type=MESH,
    ).wait()
    table = jnp.concatenate([table_ref[:, c].reshape(spots, 128) for c in range(3)], 1)
    high, low = halves(table)
    incoming = dot(jnp.concatenate([gather, gather], 1), jnp.concatenate([high, low], 0))
    low_lane = iota((entries, 128), 1) < 64
    spaced = []
    for c in range(3):
        part = incoming[:, c * 128 : c * 128 + 128]
        part = jnp.where(straight, part, pltpu.roll(part, 64, 1))
        top = part.astype(BF16).astype(F32)
        spaced.append(jnp.concatenate([jnp.where(low_lane, top, part - top), top], 1).astype(BF16))
    spaced = jnp.concatenate(spaced, 0)
    total = [0.0] * 3
    for p in range(blocks // 4):
        product = dot(spaced, weight_ref[pl.ds(256 * p, 256)], NT)
        for half in range(2):
            mask = chosen_ref[:, pl.ds(256 * p + 128 * half, 128)]
            for c in range(3):
                total[c] = total[c] + mask * product[
                    c * entries : (c + 1) * entries, 128 * half : 128 * half + 128
                ]
    stack = []
    for c in range(3):
        value = total[c][:pairs] + total[c][pairs:]
        value = value + pltpu.roll(value, 64, 1)
        top = value.astype(BF16).astype(F32)
        stack += [top, value - top]
    stack = jnp.concatenate(stack, 0).astype(BF16)
    take = jnp.where(iota((64, 128), 1) == iota((64, 128), 0), 1.0, 0.0).astype(BF16)
    turned = dot(take, stack, NT).astype(BF16)
    for c in range(3):
        lefts_ref[pl.ds(64 * c, 64), pl.ds(0, entries)] = turned[:, c * entries : (c + 1) * entries]

    for k in range(layers // 2):
        change = dot(lefts_ref[...], spread_ref[:, pl.ds(k * tall * width, tall * width)])
        for c in range(3):
            for j in range(tall):
                for z in range(8):
                    spot = pl.ds((c * depth + 8 * k + z) * height + 8 * j, 8)
                    row = 64 * c + 8 * z
                    pre_ref[spot, :] = (
                        pre_ref[spot, :] + change[row : row + 8, j * width : j * width + width]
                    )

    z_at = iota((depth, width), 0)
    z8 = z_at & 7
    z_low = (z8 == 0) & (z_at > 0)
    z_high = (z8 == 7) & (z_at < depth - 1)
    for b in range(2):

        @pl.when(has_y[b])
        def _(b=b):
            pltpu.make_async_remote_copy(
                src_ref=row_ref.at[b],
                dst_ref=row_in_ref.at[b],
                send_sem=row_send.at[b],
                recv_sem=row_recv.at[b],
                device_id={"gy": gy + 2 * b - 1},
                device_id_type=MESH,
            ).wait()
            j = b * (tall - 1)
            keep = jnp.concatenate(
                [
                    jnp.broadcast_to(
                        0.5 * scale * factor[:, (k * tall + j) * width : (k * tall + j + 1) * width],
                        (8, width),
                    )
                    for k in range(layers)
                ],
                0,
            )
            for c in range(3):
                value = jnp.concatenate([row_in_ref[b, at, c] for at in range(groups)], 0)
                near = jnp.where(
                    z_low, pltpu.roll(value, 1, 0), pltpu.roll(value, depth - 1, 0)
                )
                value = jnp.where(z_low | z_high, 0.5 * (value + near), value)
                spot = (pl.ds(c * depth * height + b * (height - 1), depth, stride=height), slice(None))
                pre_ref[spot] = pre_ref[spot] + keep * value


def finish_kernel(pre_ref, lefts_ref, spread_ref, out_hbm, out_ref, out_sem):
    _, depth, height, width = out_ref.shape
    layers, tall = depth // 8, height // 8
    first = pl.ds(0, layers // 2 * 8)
    pltpu.make_async_copy(pre_ref.at[:, first], out_hbm.at[:, first], out_sem).start()
    for k in range(layers // 2, layers):
        change = dot(lefts_ref[...], spread_ref[:, pl.ds(k * tall * width, tall * width)])
        span = pl.ds(8 * k, 8)
        for c in range(3):
            for j in range(tall):
                spot = (c, span, pl.ds(8 * j, 8))
                out_ref[spot] = pre_ref[spot] + change[
                    64 * c : 64 * c + 64, j * width : j * width + width
                ].reshape(8, 8, width)
        pltpu.make_async_copy(out_ref.at[:, span], out_hbm.at[:, span], out_sem).start()
    pltpu.make_async_copy(pre_ref, out_hbm, out_sem).wait()


def local(initial, sectioned, rotor_faces, intersections, live_counts, mortar_blocks):
    across = lax.axis_size("gx")
    along = lax.axis_size("gy")
    _, depth, height, width = sectioned.shape
    ops, face = operators(height, width)
    plane = 8 * height
    layers = depth // 8
    columns = layers * (height // 8) * width
    group = 2 if layers % 2 == 0 else 1
    groups = layers // group
    packed = rotor_faces.shape[1] // 2
    entries = intersections.shape[1]
    blocks = mortar_blocks.shape[0]
    room = 4 * int(np.prod(sectioned.shape))
    room += 2 * (3 * 64 + columns) * (entries + 128)
    hbm, vmem = pl.BlockSpec(memory_space=pltpu.HBM), pl.BlockSpec(memory_space=pltpu.VMEM)
    pre, lefts, spread = pl.pallas_call(
        functools.partial(step_kernel, across, along),
        out_shape=[
            pltpu.VMEM((3 * depth * height, width), F32),
            pltpu.VMEM((3 * 64, entries + 128), BF16),
            pltpu.VMEM((entries + 128, columns), BF16),
        ],
        in_specs=[hbm] * 3 + [pl.BlockSpec(memory_space=pltpu.SMEM)] + [hbm] * 4,
        out_specs=[vmem] * 3,
        scratch_shapes=[
            pltpu.VMEM(initial.shape, F32),
            pltpu.VMEM(sectioned.shape, F32),
            pltpu.VMEM(rotor_faces.shape, jnp.int32),
            pltpu.VMEM((3, 1, entries), jnp.int32),
            pltpu.VMEM(mortar_blocks.shape, F32),
            pltpu.VMEM(ops.shape, BF16),
            pltpu.VMEM(face.shape, BF16),
            pltpu.SemaphoreType.DMA((3,)),
            pltpu.SemaphoreType.DMA((groups,)),
            pltpu.VMEM((across, 3, packed, 128), F32),
            pltpu.VMEM((64 * blocks, 256), BF16),
            pltpu.VMEM((entries, 64 * blocks), F32),
            pltpu.VMEM((3, layers, plane, 2 * width), BF16),
            pltpu.VMEM((3, groups, face.shape[0], group * plane), F32),
            pltpu.VMEM((3 * (rotor_faces.shape[1] + 16), 3 * plane), F32),
            pltpu.VMEM((3, 3, rotor_faces.shape[1] + 16, plane), F32),
            pltpu.VMEM((groups, 3, 3 * plane, group * width), F32),
            pltpu.VMEM((groups, 3, group * plane, 2 * width), F32),
            pltpu.VMEM((3 * depth * height, width), F32),
            pltpu.VMEM((2, 4, 8, 128), F32),
            pltpu.VMEM((2, 5, 8, 128), F32),
            pltpu.VMEM((2, groups, 3, group * 8, width), F32),
            pltpu.VMEM((2, groups, 3, group * 8, width), F32),
            pltpu.SemaphoreType.DMA((2,)),
            pltpu.SemaphoreType.DMA((2,)),
            pltpu.SemaphoreType.DMA((2,)),
            pltpu.SemaphoreType.DMA((2,)),
            pltpu.SemaphoreType.DMA((2,)),
        ],
        compiler_params=pltpu.CompilerParams(
            collective_id=0, has_side_effects=True, vmem_limit_bytes=67043328 - room
        ),
        name="step",
    )(
        sectioned,
        rotor_faces,
        jnp.transpose(intersections, (2, 0, 1)),
        live_counts,
        mortar_blocks,
        jnp.asarray(ops),
        jnp.asarray(face),
        initial,
    )
    return pl.pallas_call(
        finish_kernel,
        out_shape=jax.ShapeDtypeStruct(sectioned.shape, F32),
        in_specs=[vmem] * 3,
        out_specs=hbm,
        scratch_shapes=[pltpu.VMEM(sectioned.shape, F32), pltpu.SemaphoreType.DMA],
        compiler_params=pltpu.CompilerParams(vmem_limit_bytes=32 * 1024 * 1024),
        name="finish",
    )(pre.reshape(sectioned.shape), lefts, spread)


def solution(mesh):
    return jax.shard_map(
        local,
        mesh=mesh,
        in_specs=(
            P(None, None, "gy", "gx"),
            P(None, None, "gy", "gx"),
            P("gy", "gx"),
            P("gy", "gx", None),
            P("gy", "gx"),
            P(),
        ),
        out_specs=P(None, None, "gy", "gx"),
        check_vma=False,
    )
```
